256 devices in a mesh: gx: 64 (over y, z, core), gy: 4 (over x).
Axes of the slice: x: 4, y: 4, z: 8, core: 2. Of those that a mesh axis runs over, the one named last changes fastest.
Arguments:
- members_state: float32 [3, 64, 512, 512], P(None, None, 'gx', 'gy'), may hold values from -6 to 6
- depth_level: int32 [512, 512], P('gx', 'gy'), may hold values from 1 to 8
- land_mask: int32 [512, 512], P('gx', 'gy'), may hold values 0 or 1
- obs_cells: int32 [64, 4, 256], P('gx', 'gy'), may hold values from 0 to 1023
- obs_values: float32 [64, 4, 256], P('gx', 'gy'), may hold values from -6 to 6
- obs_error: float32 [64, 4, 256], P('gx', 'gy'), may hold values from 2 to 8
Outputs:
- analysis: float32 [3, 64, 512, 512], P(None, None, 'gx', 'gy')
The draws below stay inside these ranges and needn't reach their ends.
Inputs may be any that keep to these rules, and one draw needn't show every extreme that they name: Each value of obs_cells is the row-major index of a cell within the 8 x 128 block held by the device at the same position along gx and gy.
All inputs are finite; a program needn't handle non-finite values. No bound on the sum of `land_mask` on one device may be relied on, other than what follows from the above.
Results may differ from the reference program's by a relative error of at most 0.00005.
Values sent between devices are 32-bit elements; how exact they have to be, the bound alone decides.
No kernel may reach another device: no remote copies, remote signals or barrier semaphores. Data moves between devices by JAX's collectives and lax.ppermute only.
A program may use at most 64 MiB of HBM per device.

```python
import math
import jax
import jax.numpy as jnp
from jax import lax

MEMBERS = 64
CX = 8
CY = 128
OBS = 256
NX = 512
NY = 512
N_GX = 64
N_GY = 4


def plant(drawn, stream_key, smallest, high):
    extent = drawn.shape
    index_at = [jax.random.randint(jax.random.fold_in(stream_key, axis), (), 0, extent[axis]) for axis in range(len(extent))]
    drawn = drawn.at[tuple(index_at)].set(smallest)
    longest = extent.index(max(extent))
    index_at[longest] = (index_at[longest] + 1) % extent[longest]
    return drawn.at[tuple(index_at)].set(high)


def steps_of(own_key, shape, shards, smallest, largest):
    factor_of, own = 1.0, jax.random.fold_in(own_key, 6)
    for axis_at, blocks in shards:
        steps = jnp.exp(jax.random.uniform(jax.random.fold_in(own, axis_at), (blocks,), jnp.float32, smallest / len(shards), largest / len(shards)))
        factor_of = factor_of * jnp.repeat(steps, shape[axis_at] // blocks).reshape([-1 if axis == axis_at else 1 for axis in range(len(shape))])
    return factor_of


def noise(own_key, shape, spread, limit, pieces=(), held_as=jnp.bfloat16):
    result = spread * jax.random.normal(own_key, shape, jnp.float32)
    if pieces:
        result = result * steps_of(own_key, shape, pieces, -0.22, 0.18)
    return jnp.clip(result, -limit, limit).astype(held_as)


def setup_inputs(seed: int = 0) -> dict:
    streams_of = jax.random.split(jax.random.key(seed), 7)
    members_state = noise(streams_of[0], (3, MEMBERS, NX, NY), 1.0, 6.0, ((2, 64), (3, 4)), jnp.float32)
    depth_level = plant(jax.random.randint(streams_of[1], (NX, NY), 1, 9), jax.random.fold_in(streams_of[1], 1), 1, 8).astype(jnp.int32)
    land_mask = plant((jax.random.randint(streams_of[2], (NX, NY), 0, 8) < 7).astype(jnp.int32), jax.random.fold_in(streams_of[2], 1), 0, 1)
    obs_cells = plant(jax.random.randint(streams_of[3], (N_GX, N_GY, OBS), 0, CX * CY), jax.random.fold_in(streams_of[3], 1), 0, (CX * CY) - 1).astype(jnp.int32)
    obs_values = noise(streams_of[4], (N_GX, N_GY, OBS), 1.0, 6.0, ((0, 64), (1, 4)), jnp.float32)
    obs_error = jnp.clip(jnp.exp(math.log(8.0) - 1.3862944 * jax.random.uniform(streams_of[5], (N_GX, N_GY, OBS), jnp.float32) ** steps_of(streams_of[5], (N_GX, N_GY, OBS), ((0, 64), (1, 4)), -0.2, 0.2)), 2.0, 8.0)
    return dict(members_state=members_state, depth_level=depth_level, land_mask=land_mask, obs_cells=obs_cells, obs_values=obs_values, obs_error=obs_error)


def height_tendency(padded, geo):
    h = padded[0]
    u = padded[1]
    v = padded[2]
    depth = geo[0]
    mask = geo[1][1:-1, 1:-1]
    east = depth * u
    north = depth * v

    def along_x(a):
        return (a[:, 2:, 1:-1] - a[:, :-2, 1:-1]) * 0.5

    def along_y(a):
        return (a[:, 1:-1, 2:] - a[:, 1:-1, :-2]) * 0.5

    def laplace(a):
        return a[:, 2:, 1:-1] + a[:, :-2, 1:-1] + a[:, 1:-1, 2:] + a[:, 1:-1, :-2] - 4.0 * a[:, 1:-1, 1:-1]

    def inner(a):
        return a[:, 1:-1, 1:-1]
    dh = -along_x(east) - along_y(north) + 0.05 * laplace(h)
    du = -along_x(h) + 0.2 * inner(v) + 0.05 * laplace(u)
    dv = -along_y(h) - 0.2 * inner(u) + 0.05 * laplace(v)
    return jnp.stack([dh, du, dv]) * mask

def tri_solve(lower, rhs, flipped):
    return lax.linalg.triangular_solve(lower, rhs, left_side=True, lower=True, transpose_a=flipped)

def reference(members_state, depth_level, land_mask, obs_cells, obs_values, obs_error):
    maskf = land_mask.astype(jnp.float32)
    geo = jnp.stack([0.25 * depth_level.astype(jnp.float32) * maskf, maskf])
    geo_pad = jnp.pad(geo, ((0, 0), (1, 1), (1, 1)))

    def map_through_observer(x):
        return height_tendency(jnp.pad(x, ((0, 0), (0, 0), (1, 1), (1, 1))), geo_pad)
    first_offset = members_state * maskf
    s1 = first_offset + 0.3 * map_through_observer(first_offset)
    variance_estimate2 = 0.75 * first_offset + 0.25 * (s1 + 0.3 * map_through_observer(s1))
    prior_model_vector = 1.0 / 3.0 * first_offset + 2.0 / 3.0 * (variance_estimate2 + 0.3 * map_through_observer(variance_estimate2))
    sample_average = lax.optimization_barrier(jnp.mean(prior_model_vector, axis=1, keepdims=True))
    sample_deviations = prior_model_vector - sample_average
    sample_number = prior_model_vector.shape[1]
    block_x = jnp.arange(N_GX, dtype=jnp.int32)[:, None, None] * CX
    block_y = jnp.arange(N_GY, dtype=jnp.int32)[None, :, None] * CY
    horizontal_sum_across = (block_x + obs_cells // CY).reshape(-1)
    vertical_sum_across = (block_y + obs_cells % CY).reshape(-1)
    measured_data = prior_model_vector[0][:, horizontal_sum_across, vertical_sum_across]
    obs_mean = lax.optimization_barrier(jnp.mean(measured_data, axis=0, keepdims=True))
    error = obs_error.reshape(-1)
    scaled = (measured_data - obs_mean) / (error * jnp.sqrt(jnp.float32(sample_number - 1)))
    innovation = (obs_values.reshape(-1) - obs_mean[0]) / error
    gram = jnp.dot(scaled, scaled.T, precision=lax.Precision.HIGHEST)
    projection = jnp.dot(scaled, innovation, precision=lax.Precision.HIGHEST)
    eye = jnp.eye(sample_number, dtype=jnp.float32)
    lower = jnp.linalg.cholesky(eye + gram)
    half = tri_solve(lower, projection[:, None], False)
    weights = tri_solve(lower, half, True)[:, 0]
    inverse = tri_solve(lower, eye, False)
    transform = weights[:, None] / jnp.sqrt(jnp.float32(sample_number - 1)) + inverse.T
    mixed = jnp.einsum('km,fkxy->fmxy', transform, sample_deviations, precision=lax.Precision.HIGHEST)
    return sample_average + mixed
```

```python
import jax
import jax.numpy as jnp
from jax import lax
from jax.sharding import PartitionSpec as P


def extended(block, sides, width):
    for axis, dim in sides:
        count = lax.axis_size(axis)
        forward = [(i, i + 1) for i in range(count - 1)]
        backward = [(target, source) for source, target in forward]
        low = lax.ppermute(
            lax.slice_in_dim(block, block.shape[dim] - width, None, axis=dim), axis, forward
        )
        high = lax.ppermute(lax.slice_in_dim(block, 0, width, axis=dim), axis, backward)
        block = jnp.concatenate([low, block, high], axis=dim)
    return block


def height_tendency(padded, geo):
    h = padded[0]
    u = padded[1]
    v = padded[2]
    depth = geo[0]
    mask = geo[1][1:-1, 1:-1]
    east = depth * u
    north = depth * v

    def along_x(a):
        return (a[:, 2:, 1:-1] - a[:, :-2, 1:-1]) * 0.5

    def along_y(a):
        return (a[:, 1:-1, 2:] - a[:, 1:-1, :-2]) * 0.5

    def laplace(a):
        return (
            a[:, 2:, 1:-1]
            + a[:, :-2, 1:-1]
            + a[:, 1:-1, 2:]
            + a[:, 1:-1, :-2]
            - 4.0 * a[:, 1:-1, 1:-1]
        )

    def inner(a):
        return a[:, 1:-1, 1:-1]

    dh = -along_x(east) - along_y(north) + 0.05 * laplace(h)
    du = -along_x(h) + 0.2 * inner(v) + 0.05 * laplace(u)
    dv = -along_y(h) - 0.2 * inner(u) + 0.05 * laplace(v)
    return jnp.stack([dh, du, dv]) * mask


def tri_solve(lower, rhs, flipped):
    return lax.linalg.triangular_solve(lower, rhs, left_side=True, lower=True, transpose_a=flipped)


def summed(part):
    for axis, flips in (("gx", (1,)), ("gy", (1, 3)), ("gx", (16, 48, 2, 4, 12))):
        count = lax.axis_size(axis)
        for flip in flips:
            part = part + lax.ppermute(part, axis, [(i, i ^ flip) for i in range(count)])
    return part


def padded_section(field):
    return extended(field, (("gx", 2), ("gy", 3)), 1)


def local(members_state, depth_level, land_mask, obs_cells, obs_values, obs_error):
    maskf = land_mask.astype(jnp.float32)
    geo = jnp.stack([0.25 * depth_level.astype(jnp.float32) * maskf, maskf])
    geo_wide = extended(geo, (("gx", 1), ("gy", 2)), 3)
    first_offset = members_state * maskf
    single_geometry = geo_wide[:, 2:-2, 2:-2]
    s1 = first_offset + 0.3 * height_tendency(padded_section(first_offset), single_geometry)
    variance_estimate2 = 0.75 * first_offset + 0.25 * (
        s1 + 0.3 * height_tendency(padded_section(s1), single_geometry)
    )
    prior_model_vector = 1.0 / 3.0 * first_offset + 2.0 / 3.0 * (
        variance_estimate2
        + 0.3 * height_tendency(padded_section(variance_estimate2), single_geometry)
    )
    sample_average = jnp.mean(prior_model_vector, axis=1, keepdims=True)
    sample_deviations = prior_model_vector - sample_average
    sample_number = prior_model_vector.shape[1]
    free_elevation_field = prior_model_vector[0].reshape(sample_number, -1)
    measured_data = jnp.take(free_elevation_field, obs_cells.reshape(-1), axis=1)
    obs_mean = jnp.mean(measured_data, axis=0, keepdims=True)
    error = obs_error.reshape(-1)
    scaled = (measured_data - obs_mean) / (error * jnp.sqrt(jnp.float32(sample_number - 1)))
    innovation = (obs_values.reshape(-1) - obs_mean[0]) / error
    gram_part = jnp.dot(scaled, scaled.T, precision=lax.Precision.HIGHEST)
    proj_part = jnp.dot(scaled, innovation, precision=lax.Precision.HIGHEST)
    eye = jnp.eye(sample_number, dtype=jnp.float32)
    both = summed(jnp.concatenate([gram_part, proj_part[:, None]], axis=1))
    gram, projection = both[:, :sample_number], both[:, sample_number]
    lower = jnp.linalg.cholesky(eye + gram)
    half = tri_solve(lower, projection[:, None], False)
    weights = tri_solve(lower, half, True)[:, 0]
    inverse = tri_solve(lower, eye, False)
    transform = weights[:, None] / jnp.sqrt(jnp.float32(sample_number - 1)) + inverse.T
    mixed = jnp.einsum(
        "km,fkxy->fmxy", transform, sample_deviations, precision=lax.Precision.HIGHEST
    )
    return sample_average + mixed


def solution(mesh):
    placed = (
        P(None, None, "gx", "gy"),
        P("gx", "gy"),
        P("gx", "gy"),
        P("gx", "gy", None),
        P("gx", "gy", None),
        P("gx", "gy", None),
    )
    return jax.shard_map(
        local, mesh=mesh, in_specs=placed, out_specs=P(None, None, "gx", "gy"), check_vma=False
    )
```

```python
import jax
import jax.numpy as jnp
import numpy as np
from jax import lax
from jax.experimental import pallas as pl
from jax.experimental.pallas import tpu as pltpu
from jax.sharding import PartitionSpec as P

F32 = jnp.float32
BF16 = jnp.bfloat16
MEMBERS = 64
BLOCKS = 8
ROWS = 8
COLS = 128
HALO = 3
EXT = ROWS + 2 * HALO
WIDE = 9
OBS = 256
FIELDS = 3
EDGE = FIELDS * HALO * MEMBERS


def vmem(count):
    return [pl.BlockSpec(memory_space=pltpu.VMEM)] * count


def lanes():
    return lax.broadcasted_iota(jnp.int32, (8, COLS), 1)


def turn(value, shift):
    shift = shift % COLS
    return value if shift == 0 else pltpu.roll(value, shift, 1)


def spread(row):
    return jnp.broadcast_to(row, (8, COLS))


def arrange(x_ref, depth_ref, land_ref, start_ref, geo_ref, near_ref, far_ref):
    odd = lax.rem(lax.axis_index("gx"), 2)
    land = land_ref[...].astype(F32)
    geo_ref[0] = 0.125 * depth_ref[...].astype(F32) * land
    geo_ref[1] = land
    for f in range(FIELDS):
        for r in range(ROWS):
            value = x_ref[pl.ds(f * MEMBERS * ROWS + r, MEMBERS, stride=ROWS), :]
            start_ref[f, r] = value * land[r : r + 1, :]
    low = (ROWS - HALO) * (1 - odd)
    for target, first in ((near_ref, low), (far_ref, (ROWS - HALO) - low)):
        for f in range(FIELDS):
            for r in range(HALO):
                at = (f * HALO + r) * MEMBERS
                target[at : at + MEMBERS, :] = start_ref[f, first + r]
        for g in range(2):
            for r in range(HALO):
                at = EDGE + g * HALO + r
                target[at : at + 1, :] = geo_ref[g, pl.ds(first + r, 1), :]
        target[EDGE + 6 : EDGE + 8, :] = jnp.zeros((2, COLS), F32)


def strips(start_ref, geo_ref, near_ref, far_ref, halo_ref, wide_ref, left_ref, right_ref, a_ref, b_ref):
    odd_x = lax.rem(lax.axis_index("gx"), 2) == 1
    odd_y = lax.rem(lax.axis_index("gy"), 2) == 1
    lane = lanes()
    shifted = lax.rem(lane + HALO, COLS)
    for f in range(FIELDS):
        for r in range(HALO):
            at = slice((f * HALO + r) * MEMBERS, (f * HALO + r + 1) * MEMBERS)
            near, far = near_ref[at, :], far_ref[at, :]
            halo_ref[f, r] = jnp.where(odd_x, near, far)
            halo_ref[f, HALO + r] = jnp.where(odd_x, far, near)
    near, far = near_ref[EDGE : EDGE + 8, :], far_ref[EDGE : EDGE + 8, :]
    above, below = jnp.where(odd_x, near, far), jnp.where(odd_x, far, near)
    for g in range(2):
        at = slice(g * HALO, (g + 1) * HALO)
        wide_ref[g, :HALO] = above[at]
        wide_ref[g, HALO : HALO + ROWS] = geo_ref[g]
        wide_ref[g, HALO + ROWS :] = below[at]

    def put(packed, own, f, place):
        to_left, to_right = packed
        left, right = own
        left_ref[place] = left
        right_ref[place] = right
        mine = (lax.rem(lane, WIDE) // HALO) == f
        to_left = jnp.where(mine, turn(left, HALO * f - HALO), to_left)
        to_right = jnp.where(mine, turn(right, HALO * f), to_right)
        return to_left, to_right

    def own_columns(row_of):
        left = jnp.zeros((8, COLS), F32)
        right = jnp.zeros((8, COLS), F32)
        for r in range(EXT):
            value = turn(row_of(r), WIDE * r + HALO)
            left = jnp.where((lane // WIDE == r) & (lax.rem(lane, WIDE) >= HALO), value, left)
            right = jnp.where((shifted // WIDE == r) & (lax.rem(shifted, WIDE) < 2 * HALO), value, right)
        return left, right

    def send(place, packed):
        to_left, to_right = packed
        a_ref[place] = jnp.where(odd_y, to_left, to_right)
        b_ref[place] = jnp.where(odd_y, to_right, to_left)

    def block(m, carry):
        at = pl.ds(pl.multiple_of(m * 8, 8), 8)
        packed = (jnp.zeros((8, COLS), F32),) * 2
        for f in range(FIELDS):

            def row_of(r):
                if r < HALO:
                    return halo_ref[f, r, at, :]
                if r < HALO + ROWS:
                    return start_ref[f, r - HALO, at, :]
                return halo_ref[f, r - ROWS, at, :]

            packed = put(packed, own_columns(row_of), f, f * BLOCKS + m)
        send(m, packed)
        return carry

    lax.fori_loop(0, BLOCKS, block, 0)
    packed = (jnp.zeros((8, COLS), F32),) * 2
    for g in range(2):
        packed = put(packed, own_columns(lambda r: spread(wide_ref[g, r : r + 1, :])), g, FIELDS * BLOCKS + g)
    send(BLOCKS, packed)


def section(h, u, v, depth):
    damp = 0.05 * h
    half = 0.5 * h
    east, north = depth * u, depth * v
    us, vs = 0.05 * u, 0.05 * v
    return dict(
        up=(damp - east, us - half, vs),
        down=(damp + east, us + half, vs),
        back=(damp - north, us, vs - half),
        ahead=(damp + north, us, vs + half),
        here=(-0.2 * h, 0.2 * (v - u), -0.2 * (u + v)),
    )


def tendency(up, down, back, ahead, here):
    return [a + b + c + d + e for a, b, c, d, e in zip(up, down, back, ahead, here)]


def combine(stage, first, old, change):
    new = old + change
    if stage == 0:
        return new
    if stage == 1:
        return 0.75 * first + 0.25 * new
    return (1.0 / 3.0) * first + (2.0 / 3.0) * new


def forecast(
    start_ref, halo_ref, wide_ref, left_ref, right_ref, a_ref, b_ref, cells_ref, values_ref, error_ref,
    anomaly_ref, mean_ref, part_ref, geo, s1, s2, total, seen,
):
    odd_y = lax.rem(lax.axis_index("gy"), 2) == 1
    lane = lanes()
    column = lax.rem(lane, WIDE)
    inner = (lane < HALO) | (lane >= COLS - HALO)
    for r in range(EXT):
        geo[0, r] = spread(wide_ref[0, r : r + 1, :])
        geo[1, r] = spread(0.3 * wide_ref[1, r : r + 1, :])

    def sides(place, f, own):
        a, b = a_ref[place], b_ref[place]
        from_left, from_right = jnp.where(odd_y, a, b), jnp.where(odd_y, b, a)
        left = jnp.where(column < HALO, turn(from_left, -HALO * f), left_ref[own])
        right = jnp.where(
            (column >= HALO) & (column < 2 * HALO), turn(from_right, HALO - HALO * f), right_ref[own]
        )
        return left, right

    depth_sides = sides(BLOCKS, 0, FIELDS * BLOCKS)
    land_sides = [0.3 * value for value in sides(BLOCKS, 1, FIELDS * BLOCKS + 1)]
    total[...] = jnp.zeros_like(total)
    cell = jnp.broadcast_to(cells_ref[...], (8, OBS))
    cell_row, cell_col = cell // COLS, lax.rem(cell, COLS)

    def block(m, carry):
        at = pl.ds(pl.multiple_of(m * 8, 8), 8)

        def row_of(f, r):
            if r < HALO:
                return halo_ref[f, r, at, :]
            if r < HALO + ROWS:
                return start_ref[f, r - HALO, at, :]
            return halo_ref[f, r - ROWS, at, :]

        strip = []
        fields = [sides(m, f, f * BLOCKS + m) for f in range(FIELDS)]
        for side in range(2):
            first = [fields[f][side] for f in range(FIELDS)]
            now = first
            for stage in range(3):
                part = section(*now, depth_sides[side])
                change = tendency(
                    [turn(value, -WIDE) for value in part["up"]],
                    [turn(value, WIDE) for value in part["down"]],
                    [turn(value, -1) for value in part["back"]],
                    [turn(value, 1) for value in part["ahead"]],
                    part["here"],
                )
                now = [combine(stage, first[f], now[f], land_sides[side] * change[f]) for f in range(FIELDS)]
            strip.append(now)
        edge = [jnp.where(column >= HALO, strip[0][f], strip[1][f]) for f in range(FIELDS)]

        heights = []
        for stage in range(3):
            read = row_of if stage == 0 else (lambda f, r, ref=(s1, s2)[stage - 1]: ref[f, r])
            known = {}

            def part_of(r):
                if r not in known:
                    known[r] = section(*[read(f, r) for f in range(FIELDS)], geo[0, r])
                return known[r]

            for r in range(stage + 1, EXT - stage - 1):
                mine = part_of(r)
                change = tendency(
                    part_of(r + 1)["up"],
                    part_of(r - 1)["down"],
                    [turn(value, -1) for value in mine["back"]],
                    [turn(value, 1) for value in mine["ahead"]],
                    mine["here"],
                )
                for f in range(FIELDS):
                    new = combine(stage, row_of(f, r), read(f, r), geo[1, r] * change[f])
                    if stage < 2:
                        (s1, s2)[stage][f, r] = new
                    else:
                        new = jnp.where(inner, turn(edge[f], -(WIDE * r + HALO)), new)
                        anomaly_ref[f, r - HALO, at, :] = new
                        total[f * ROWS + r - HALO] += new
                        if f == 0:
                            heights.append(new)
        for part in range(OBS // COLS):
            cut = slice(part * COLS, (part + 1) * COLS)
            got = jnp.zeros((8, COLS), F32)
            for r in range(ROWS):
                picked = jnp.take_along_axis(heights[r], cell_col[:, cut], axis=1)
                got = jnp.where(cell_row[:, cut] == r, picked, got)
            seen[at, cut] = got
        return carry

    lax.fori_loop(0, BLOCKS, block, 0)

    everything = seen[...]
    obs_mean = jnp.sum(everything, axis=0, keepdims=True) * (1.0 / MEMBERS)
    error = error_ref[...]
    scaled = (everything - obs_mean) * (1.0 / (error * np.sqrt(np.float32(MEMBERS - 1))))
    innovation = (values_ref[...] - obs_mean) / error
    product = lambda a: lax.dot_general(
        a, scaled, (((1,), (1,)), ((), ())), precision=lax.Precision.HIGHEST, preferred_element_type=F32
    )
    gram = product(scaled)
    part_ref[:32, :MEMBERS] = gram[:32]
    part_ref[:32, MEMBERS:] = gram[32:]
    part_ref[32:, :MEMBERS] = product(jnp.broadcast_to(innovation, (8, OBS)))
    part_ref[32:, MEMBERS:] = jnp.zeros((8, MEMBERS), F32)

    for k in range(FIELDS * ROWS):
        f, r = divmod(k, ROWS)
        mean = jnp.sum(total[k], axis=0, keepdims=True) * (1.0 / MEMBERS)
        mean_ref[k : k + 1, :] = mean
        anomaly_ref[f, r] = anomaly_ref[f, r] - mean


def analyse(sum_ref, anomaly_ref, mean_ref, out_ref):
    lane = lanes()
    sub = lax.broadcasted_iota(jnp.int32, (8, COLS), 0)
    table = []
    for b in range(BLOCKS):
        if b < 4:
            value = sum_ref[b * 8 : b * 8 + 8, :]
        else:
            value = turn(sum_ref[(b - 4) * 8 : (b - 4) * 8 + 8, :], MEMBERS)
        value = jnp.where(lane < MEMBERS, value, 0.0)
        one = (lane == sub + 8 * b) | (lane == sub + 8 * b + MEMBERS)
        table.append(value + jnp.where(one, 1.0, 0.0))
    pivots = [jnp.ones((8, COLS), F32) for _ in range(BLOCKS)]
    for j in range(MEMBERS):
        b, s = divmod(j, 8)
        row = spread(table[b][s : s + 1, :])
        pivot = jnp.broadcast_to(row[:, j : j + 1], (8, COLS))
        pivots[b] = jnp.where(sub == s, pivot, pivots[b])
        row = row * (1.0 / pivot)
        for i in range(b, BLOCKS):
            factor = jnp.broadcast_to(table[i][:, j : j + 1], (8, COLS))
            if i == b:
                factor = jnp.where(sub > s, factor, 0.0)
            table[i] = table[i] - factor * row
    inverse = [
        jnp.where(lane < MEMBERS, turn(table[b] * lax.rsqrt(pivots[b]), MEMBERS), 0.0) for b in range(BLOCKS)
    ]
    projection = spread(sum_ref[32:33, :])
    weights = jnp.zeros((8, COLS), F32)
    for b in range(BLOCKS):
        weights = weights + inverse[b] * jnp.sum(inverse[b] * projection, axis=1, keepdims=True)
    weights = jnp.sum(weights, axis=0, keepdims=True) / np.sqrt(np.float32(MEMBERS - 1))
    transform = jnp.concatenate(inverse, axis=0)[:, :MEMBERS] + weights[:, :MEMBERS]
    high = transform.astype(BF16)
    low = (transform - high.astype(F32)).astype(BF16)
    taps = jnp.concatenate([high, low, high], axis=1)
    for f in range(FIELDS):
        for r in range(0, ROWS, 2):
            value = jnp.concatenate([anomaly_ref[f, r], anomaly_ref[f, r + 1]], axis=1)
            big = value.astype(BF16)
            small = (value - big.astype(F32)).astype(BF16)
            mixed = jnp.dot(taps, jnp.concatenate([big, big, small], axis=0), preferred_element_type=F32)
            for q in range(2):
                k = f * ROWS + r + q
                out_ref[pl.ds(f * MEMBERS * ROWS + r + q, MEMBERS, stride=ROWS), :] = (
                    mean_ref[k : k + 1, :] + mixed[:, q * COLS : (q + 1) * COLS]
                )


def swap(value, axis, pairs):
    return lax.ppermute(value, axis, [(a, b) for a, b in pairs] + [(b, a) for a, b in pairs])


def pairs_of(count, first):
    return [(i, i + 1) for i in range(first, count - 1, 2)]


def summed(part):
    for axis, flips in (("gx", (1,)), ("gy", (1, 3)), ("gx", (16, 48, 2, 4, 12))):
        count = lax.axis_size(axis)
        for flip in flips:
            part = part + lax.ppermute(part, axis, [(i, i ^ flip) for i in range(count)])
    return part


def shape(*sizes):
    return jax.ShapeDtypeStruct(sizes, F32)


def local(members_state, depth_level, land_mask, obs_cells, obs_values, obs_error):
    x = members_state.reshape(FIELDS * MEMBERS * ROWS, COLS)
    start, geo, near, far = pl.pallas_call(
        arrange,
        out_shape=(shape(FIELDS, ROWS, MEMBERS, COLS), shape(2, ROWS, COLS), shape(EDGE + 8, COLS), shape(EDGE + 8, COLS)),
        in_specs=vmem(3),
        out_specs=tuple(vmem(4)),
        name="arrange",
    )(x, depth_level, land_mask)
    near = swap(near, "gx", pairs_of(64, 0))
    far = swap(far, "gx", pairs_of(64, 1))
    tile = shape(BLOCKS + 1, 8, COLS)
    halo, wide, left, right, a, b = pl.pallas_call(
        strips,
        out_shape=(
            shape(FIELDS, 2 * HALO, MEMBERS, COLS), shape(2, EXT, COLS),
            shape(FIELDS * BLOCKS + 2, 8, COLS), shape(FIELDS * BLOCKS + 2, 8, COLS), tile, tile,
        ),
        in_specs=vmem(4),
        out_specs=tuple(vmem(6)),
        name="strips",
    )(start, geo, near, far)
    a = swap(a, "gy", pairs_of(4, 0))
    b = swap(b, "gy", pairs_of(4, 1))
    anomaly, mean, part = pl.pallas_call(
        forecast,
        out_shape=(shape(FIELDS, ROWS, MEMBERS, COLS), shape(FIELDS * ROWS, COLS), shape(40, COLS)),
        in_specs=vmem(10),
        out_specs=tuple(vmem(3)),
        scratch_shapes=[
            pltpu.VMEM((2, EXT, 8, COLS), F32),
            pltpu.VMEM((FIELDS, EXT, 8, COLS), F32),
            pltpu.VMEM((FIELDS, EXT, 8, COLS), F32),
            pltpu.VMEM((FIELDS * ROWS, 8, COLS), F32),
            pltpu.VMEM((MEMBERS, OBS), F32),
        ],
        name="forecast",
    )(
        start, halo, wide, left, right, a, b,
        obs_cells.reshape(1, OBS), obs_values.reshape(1, OBS), obs_error.reshape(1, OBS),
    )
    out = pl.pallas_call(
        analyse,
        out_shape=shape(FIELDS * MEMBERS * ROWS, COLS),
        in_specs=vmem(3),
        out_specs=vmem(1)[0],
        name="analyse",
    )(summed(part), anomaly, mean)
    return out.reshape(FIELDS, MEMBERS, ROWS, COLS)


def solution(mesh):
    placed = (
        P(None, None, "gx", "gy"),
        P("gx", "gy"),
        P("gx", "gy"),
        P("gx", "gy", None),
        P("gx", "gy", None),
        P("gx", "gy", None),
    )
    return jax.shard_map(
        local, mesh=mesh, in_specs=placed, out_specs=P(None, None, "gx", "gy"), check_vma=False
    )
```

```python
import jax
import jax.numpy as jnp
import numpy as np
from jax import lax
from jax.experimental import pallas as pl
from jax.experimental.pallas import tpu as pltpu
from jax.sharding import PartitionSpec as P

F32 = jnp.float32
BF16 = jnp.bfloat16
MEMBERS = 64
BLOCKS = 8
ROWS = 8
COLS = 128
HALO = 3
EXT = ROWS + 2 * HALO
WIDE = 9
OBS = 256
FIELDS = 3
EDGE = FIELDS * HALO * MEMBERS


def vmem(count):
    return [pl.BlockSpec(memory_space=pltpu.VMEM)] * count


def lanes():
    return lax.broadcasted_iota(jnp.int32, (8, COLS), 1)


def grid_sub():
    return lax.broadcasted_iota(jnp.int32, (8, COLS), 0)


def turn(value, shift):
    shift = shift % COLS
    return value if shift == 0 else pltpu.roll(value, shift, 1)


def spread(row):
    return jnp.broadcast_to(row, (8, COLS))


def arrange(x_hbm, depth_hbm, land_hbm, start_ref, geo_ref, near_ref, far_ref, x_ref, depth_ref, land_ref, sems):
    size = MEMBERS * ROWS
    loads = [
        pltpu.make_async_copy(land_hbm, land_ref, sems.at[0]),
        pltpu.make_async_copy(depth_hbm, depth_ref, sems.at[1]),
    ]
    for f in range(FIELDS):
        cut = pl.ds(f * size, size)
        loads.append(pltpu.make_async_copy(x_hbm.at[cut], x_ref.at[cut], sems.at[2 + f]))
    for load in loads:
        load.start()
    odd = lax.rem(lax.axis_index("gx"), 2)
    loads[0].wait()
    loads[1].wait()
    land = land_ref[...].astype(F32)
    geo_ref[0] = 0.125 * depth_ref[...].astype(F32) * land
    geo_ref[1] = land
    low = (ROWS - HALO) * (1 - odd)
    sends = ((near_ref, low), (far_ref, (ROWS - HALO) - low))
    for target, first in sends:
        for g in range(2):
            for r in range(HALO):
                at = EDGE + g * HALO + r
                target[at : at + 1, :] = geo_ref[g, pl.ds(first + r, 1), :]
        target[EDGE + 6 : EDGE + 8, :] = jnp.zeros((2, COLS), F32)
    for f in range(FIELDS):
        loads[2 + f].wait()
        for r in range(ROWS):
            value = x_ref[pl.ds(f * size + r, MEMBERS, stride=ROWS), :]
            start_ref[f, r] = value * land[r : r + 1, :]
        for target, first in sends:
            for r in range(HALO):
                at = (f * HALO + r) * MEMBERS
                target[at : at + MEMBERS, :] = start_ref[f, first + r]


def own_columns(row_of, rows, left, right):
    lane = lanes()
    shifted = lax.rem(lane + HALO, COLS)
    for r in rows:
        value = turn(row_of(r), WIDE * r + HALO)
        left = jnp.where((lane // WIDE == r) & (lax.rem(lane, WIDE) >= HALO), value, left)
        right = jnp.where((shifted // WIDE == r) & (lax.rem(shifted, WIDE) < 2 * HALO), value, right)
    return left, right


def interior(start_ref, geo_ref, left_ref, right_ref, c1_ref, c2_ref, c3_ref, geo):
    for r in range(ROWS):
        geo[0, r] = spread(geo_ref[0, r : r + 1, :])
        geo[1, r] = spread(0.3 * geo_ref[1, r : r + 1, :])
    blank = jnp.zeros((8, COLS), F32)
    inside = range(HALO, HALO + ROWS)

    def block(m, carry):
        at = pl.ds(pl.multiple_of(m * 8, 8), 8)
        for f in range(FIELDS):
            place = f * BLOCKS + m
            left_ref[place], right_ref[place] = own_columns(
                lambda r: start_ref[f, r - HALO, at, :], inside, blank, blank
            )

        def first(f, r):
            return start_ref[f, r, at, :]

        refs = (c1_ref, c2_ref, c3_ref)
        for stage in range(3):
            read = first if stage == 0 else (lambda f, r: refs[stage - 1][f, r - stage, at, :])

            def write(f, r, new):
                refs[stage][f, r - stage - 1, at, :] = new

            advance(stage, range(stage + 1, ROWS - stage - 1), first, read, geo, write)
        return carry

    lax.fori_loop(0, BLOCKS, block, 0)
    for g in range(2):
        place = FIELDS * BLOCKS + g
        left_ref[place], right_ref[place] = own_columns(
            lambda r: spread(geo_ref[g, r - HALO : r - HALO + 1, :]), inside, blank, blank
        )


def strips(near_ref, far_ref, geo_ref, own_left, own_right, halo_ref, wide_ref, left_ref, right_ref, a_ref, b_ref):
    odd_x = lax.rem(lax.axis_index("gx"), 2) == 1
    odd_y = lax.rem(lax.axis_index("gy"), 2) == 1
    field = lax.rem(lanes(), WIDE) // HALO
    outside = tuple(range(HALO)) + tuple(range(HALO + ROWS, EXT))
    near, far = near_ref[EDGE : EDGE + 8, :], far_ref[EDGE : EDGE + 8, :]
    above, below = jnp.where(odd_x, near, far), jnp.where(odd_x, far, near)
    for g in range(2):
        at = slice(g * HALO, (g + 1) * HALO)
        wide_ref[g, :HALO] = above[at]
        wide_ref[g, HALO : HALO + ROWS] = geo_ref[g]
        wide_ref[g, HALO + ROWS :] = below[at]

    def put(packed, row_of, f, place):
        to_left, to_right = packed
        left, right = own_columns(row_of, outside, own_left[place], own_right[place])
        left_ref[place] = left
        right_ref[place] = right
        to_left = jnp.where(field == f, turn(left, HALO * f - HALO), to_left)
        to_right = jnp.where(field == f, turn(right, HALO * f), to_right)
        return to_left, to_right

    def send(place, packed):
        to_left, to_right = packed
        a_ref[place] = jnp.where(odd_y, to_left, to_right)
        b_ref[place] = jnp.where(odd_y, to_right, to_left)

    def block(m, carry):
        at = pl.ds(pl.multiple_of(m * 8, 8), 8)
        packed = (jnp.zeros((8, COLS), F32),) * 2
        for f in range(FIELDS):
            rows = {}
            for r in range(HALO):
                cut = pl.ds(pl.multiple_of((f * HALO + r) * MEMBERS + m * 8, 8), 8)
                near, far = near_ref[cut, :], far_ref[cut, :]
                rows[r] = jnp.where(odd_x, near, far)
                rows[r + ROWS + HALO] = jnp.where(odd_x, far, near)
                halo_ref[f, r, at, :] = rows[r]
                halo_ref[f, r + HALO, at, :] = rows[r + ROWS + HALO]
            packed = put(packed, rows.get, f, f * BLOCKS + m)
        send(m, packed)
        return carry

    lax.fori_loop(0, BLOCKS, block, 0, unroll=2)
    packed = (jnp.zeros((8, COLS), F32),) * 2
    for g in range(2):
        packed = put(packed, lambda r: spread(wide_ref[g, r : r + 1, :]), g, FIELDS * BLOCKS + g)
    send(BLOCKS, packed)


def section(h, u, v, depth):
    damp = 0.05 * h
    half = 0.5 * h
    east, north = depth * u, depth * v
    us, vs = 0.05 * u, 0.05 * v
    return dict(
        up=(damp - east, us - half, vs),
        down=(damp + east, us + half, vs),
        back=(damp - north, us, vs - half),
        ahead=(damp + north, us, vs + half),
        here=(-0.2 * h, 0.2 * (v - u), -0.2 * (u + v)),
    )


def tendency(up, down, back, ahead, here):
    return [a + b + c + d + e for a, b, c, d, e in zip(up, down, back, ahead, here)]


def combine(stage, first, old, change):
    new = old + change
    if stage == 0:
        return new
    if stage == 1:
        return 0.75 * first + 0.25 * new
    return (1.0 / 3.0) * first + (2.0 / 3.0) * new


def advance(stage, rows, first, read, geo, write):
    known = {}

    def part_of(r):
        if r not in known:
            known[r] = section(*[read(f, r) for f in range(FIELDS)], geo[0, r])
        return known[r]

    for r in rows:
        mine = part_of(r)
        change = tendency(
            part_of(r + 1)["up"],
            part_of(r - 1)["down"],
            [turn(value, -1) for value in mine["back"]],
            [turn(value, 1) for value in mine["ahead"]],
            mine["here"],
        )
        for f in range(FIELDS):
            write(f, r, combine(stage, first(f, r), read(f, r), geo[1, r] * change[f]))


OUTER = tuple(range(HALO)) + tuple(range(ROWS - HALO, ROWS))


def outer(start_ref, halo_ref, wide_ref, c1_ref, c2_ref, last_ref, geo, s1, s2):
    for r in range(EXT):
        geo[0, r] = spread(wide_ref[0, r : r + 1, :])
        geo[1, r] = spread(0.3 * wide_ref[1, r : r + 1, :])

    def block(m, carry):
        at = pl.ds(pl.multiple_of(m * 8, 8), 8)

        def first(f, r):
            if r < HALO:
                return halo_ref[f, r, at, :]
            if r < HALO + ROWS:
                return start_ref[f, r - HALO, at, :]
            return halo_ref[f, r - ROWS, at, :]

        for stage in range(3):

            def read(f, r):
                if stage == 0:
                    return first(f, r)
                inside = HALO + stage
                if inside <= r < EXT - inside:
                    return (c1_ref, c2_ref)[stage - 1][f, r - inside, at, :]
                return (s1, s2)[stage - 1][f, r]

            def write(f, r, new):
                if stage < 2:
                    (s1, s2)[stage][f, r] = new
                else:
                    last_ref[f, OUTER.index(r - HALO), at, :] = new

            low, high = stage + 1, stage + 1 + HALO
            advance(stage, range(low, high), first, read, geo, write)
            advance(stage, range(EXT - high, EXT - low), first, read, geo, write)
        return carry

    lax.fori_loop(0, BLOCKS, block, 0)


def final_row(f, r, at, inner_ref, outer_ref):
    return outer_ref[f, OUTER.index(r), at, :] if r in OUTER else inner_ref[f, r - HALO, at, :]


def mended(edge, r, value):
    lane = lanes()
    border = (lane < HALO) | (lane >= COLS - HALO)
    return jnp.where(border, turn(edge, -(WIDE * (r + HALO) + HALO)), value)


def observe(
    wide_ref, left_ref, right_ref, a_ref, b_ref, inner_ref, outer_ref, cells_hbm, values_hbm, error_hbm,
    edge_ref, part_ref, seen, cells_ref, values_ref, error_ref, sems,
):
    loads = [
        pltpu.make_async_copy(source, target, sems.at[i])
        for i, (source, target) in enumerate(
            ((cells_hbm, cells_ref), (values_hbm, values_ref), (error_hbm, error_ref))
        )
    ]
    for load in loads:
        load.start()
    odd_y = lax.rem(lax.axis_index("gy"), 2) == 1
    column = lax.rem(lanes(), WIDE)

    def sides(place, f, own):
        a, b = a_ref[place], b_ref[place]
        from_left, from_right = jnp.where(odd_y, a, b), jnp.where(odd_y, b, a)
        left = jnp.where(column < HALO, turn(from_left, -HALO * f), left_ref[own])
        right = jnp.where(
            (column >= HALO) & (column < 2 * HALO), turn(from_right, HALO - HALO * f), right_ref[own]
        )
        return left, right

    depth_sides = sides(BLOCKS, 0, FIELDS * BLOCKS)
    land_sides = [0.3 * value for value in sides(BLOCKS, 1, FIELDS * BLOCKS + 1)]

    def strip(m, carry):
        fields = [sides(m, f, f * BLOCKS + m) for f in range(FIELDS)]
        done = []
        for side in range(2):
            first = [fields[f][side] for f in range(FIELDS)]
            now = first
            for stage in range(3):
                part = section(*now, depth_sides[side])
                change = tendency(
                    [turn(value, -WIDE) for value in part["up"]],
                    [turn(value, WIDE) for value in part["down"]],
                    [turn(value, -1) for value in part["back"]],
                    [turn(value, 1) for value in part["ahead"]],
                    part["here"],
                )
                now = [combine(stage, first[f], now[f], land_sides[side] * change[f]) for f in range(FIELDS)]
            done.append(now)
        for f in range(FIELDS):
            edge_ref[f, m] = jnp.where(column >= HALO, done[0][f], done[1][f])
        return carry

    lax.fori_loop(0, BLOCKS, strip, 0, unroll=2)
    for load in loads:
        load.wait()
    cell = jnp.broadcast_to(cells_ref[...], (8, OBS))
    cell_row, cell_col = cell // COLS, lax.rem(cell, COLS)

    def look(m, carry):
        at = pl.ds(pl.multiple_of(m * 8, 8), 8)
        edge = edge_ref[0, m]
        heights = [mended(edge, r, final_row(0, r, at, inner_ref, outer_ref)) for r in range(ROWS)]
        for part in range(OBS // COLS):
            cut = slice(part * COLS, (part + 1) * COLS)
            got = jnp.zeros((8, COLS), F32)
            for r in range(ROWS):
                picked = jnp.take_along_axis(heights[r], cell_col[:, cut], axis=1)
                got = jnp.where(cell_row[:, cut] == r, picked, got)
            seen[at, cut] = got
        return carry

    lax.fori_loop(0, BLOCKS, look, 0, unroll=2)
    everything = seen[...]
    obs_mean = jnp.sum(everything, axis=0, keepdims=True) * (1.0 / MEMBERS)
    error = error_ref[...]
    scaled = (everything - obs_mean) * (1.0 / (error * np.sqrt(np.float32(MEMBERS - 1))))
    innovation = (values_ref[...] - obs_mean) / error
    product = lax.dot_general(
        jnp.concatenate([scaled, jnp.broadcast_to(innovation, (8, OBS))], axis=0),
        scaled,
        (((1,), (1,)), ((), ())),
        precision=lax.Precision.HIGHEST,
        preferred_element_type=F32,
    )
    part_ref[:32, :MEMBERS] = product[:32]
    part_ref[:32, MEMBERS:] = product[32:MEMBERS]
    part_ref[32:, :MEMBERS] = product[MEMBERS:]
    part_ref[32:, MEMBERS:] = jnp.zeros((8, MEMBERS), F32)


def deviate(edge_ref, inner_ref, outer_ref, big_ref, small_ref, mean_ref):
    for f in range(FIELDS):
        for r in range(ROWS):
            rows = []
            for m in range(BLOCKS):
                at = slice(m * 8, m * 8 + 8)
                rows.append(mended(edge_ref[f, m], r, final_row(f, r, at, inner_ref, outer_ref)))
            value = jnp.concatenate(rows, axis=0)
            mean = jnp.sum(value, axis=0, keepdims=True) * (1.0 / MEMBERS)
            k = f * ROWS + r
            mean_ref[k : k + 1, :] = mean
            value = value - mean
            big = value.astype(BF16)
            big_ref[f, r] = big
            small_ref[f, r] = (value - big.astype(F32)).astype(BF16)


def column_of(value, j):
    return jnp.broadcast_to(value[:, j : j + 1], (8, COLS))


def inverse_factor(sum_ref):
    lane, sub = lanes(), grid_sub()
    table = []
    for b in range(BLOCKS):
        at = (b % 4) * 8
        value = turn(sum_ref[at : at + 8, :], MEMBERS * (b // 4))
        one = (lane == sub + 8 * b) | (lane == sub + 8 * b + MEMBERS)
        table.append(jnp.where(lane < MEMBERS, value, 0.0) + jnp.where(one, 1.0, 0.0))
    for b in range(BLOCKS):
        rows = [spread(table[b][s : s + 1, :]) for s in range(8)]
        entry = {(s, t): column_of(rows[s], 8 * b + t) for s in range(8) for t in range(s, 8)}
        over = []
        for s in range(8):
            over.append(1.0 / entry[s, s])
            for t in range(s + 1, 8):
                factor = entry[s, t] * over[s]
                for q in range(t, 8):
                    entry[t, q] = entry[t, q] - factor * entry[s, q]
                rows[t] = rows[t] - factor * rows[s]
        for i in range(b + 1, BLOCKS):
            column = [column_of(table[i], 8 * b + s) for s in range(8)]
            for s in range(8):
                column[s] = column[s] * over[s]
                for t in range(s + 1, 8):
                    column[t] = column[t] - column[s] * entry[s, t]
                table[i] = table[i] - column[s] * rows[s]
        for s in range(8):
            table[b] = jnp.where(sub == s, rows[s] * lax.rsqrt(entry[s, s]), table[b])
    return [jnp.where(lane < MEMBERS, turn(value, MEMBERS), 0.0) for value in table]


def analyse(sum_ref, big_ref, small_ref, mean_ref, out_hbm, out_ref, sems):
    inverse = inverse_factor(sum_ref)
    projection = spread(sum_ref[32:33, :])
    weights = jnp.zeros((8, COLS), F32)
    for b in range(BLOCKS):
        weights = weights + inverse[b] * jnp.sum(inverse[b] * projection, axis=1, keepdims=True)
    weights = jnp.sum(weights, axis=0, keepdims=True) / np.sqrt(np.float32(MEMBERS - 1))
    transform = jnp.concatenate(inverse, axis=0)[:, :MEMBERS] + weights[:, :MEMBERS]
    high = transform.astype(BF16)
    low = (transform - high.astype(F32)).astype(BF16)
    taps = jnp.concatenate([high, low, high], axis=1)
    stores = []
    for f in range(FIELDS):
        for r in range(0, ROWS, 2):
            big = jnp.concatenate([big_ref[f, r], big_ref[f, r + 1]], axis=1)
            small = jnp.concatenate([small_ref[f, r], small_ref[f, r + 1]], axis=1)
            mixed = jnp.dot(taps, jnp.concatenate([big, big, small], axis=0), preferred_element_type=F32)
            for q in range(2):
                k = f * ROWS + r + q
                out_ref[pl.ds(f * MEMBERS * ROWS + r + q, MEMBERS, stride=ROWS), :] = (
                    mean_ref[k : k + 1, :] + mixed[:, q * COLS : (q + 1) * COLS]
                )
        cut = pl.ds(f * MEMBERS * ROWS, MEMBERS * ROWS)
        stores.append(pltpu.make_async_copy(out_ref.at[cut], out_hbm.at[cut], sems.at[f]))
        stores[-1].start()
    for store in stores:
        store.wait()


def swap(value, axis, pairs):
    return lax.ppermute(value, axis, [(a, b) for a, b in pairs] + [(b, a) for a, b in pairs])


def pairs_of(count, first):
    return [(i, i + 1) for i in range(first, count - 1, 2)]


def summed(part):
    for axis, flips in (("gx", (1,)), ("gy", (1, 3)), ("gx", (16, 48, 2, 4, 12))):
        count = lax.axis_size(axis)
        for flip in flips:
            part = part + lax.ppermute(part, axis, [(i, i ^ flip) for i in range(count)])
    return part


def shape(*sizes, dtype=F32):
    return jax.ShapeDtypeStruct(sizes, dtype)


def hbm(count):
    return [pl.BlockSpec(memory_space=pltpu.HBM)] * count


def call(body, outs, ins, scratch=(), out_specs=None, moved=2 * 2**20):
    return pl.pallas_call(
        body,
        out_shape=outs,
        in_specs=ins,
        out_specs=out_specs or tuple(vmem(len(outs))),
        scratch_shapes=scratch,
        name=body.__name__,
        compiler_params=pltpu.CompilerParams(vmem_limit_bytes=8 * 2**20),
        cost_estimate=pl.CostEstimate(flops=0, transcendentals=0, bytes_accessed=moved),
    )


def local(members_state, depth_level, land_mask, obs_cells, obs_values, obs_error):
    x = members_state.reshape(FIELDS * MEMBERS * ROWS, COLS)
    dma = pltpu.SemaphoreType.DMA
    payload = shape(EDGE + 8, COLS)
    start, geo, near, far = call(
        arrange,
        (shape(FIELDS, ROWS, MEMBERS, COLS), shape(2, ROWS, COLS), payload, payload),
        hbm(3),
        [
            pltpu.VMEM(x.shape, F32), pltpu.VMEM((ROWS, COLS), jnp.int32), pltpu.VMEM((ROWS, COLS), jnp.int32),
            dma((5,)),
        ],
    )(*[pltpu.with_memory_space_constraint(value, pltpu.HBM) for value in (x, depth_level, land_mask)])
    far = swap(far, "gx", pairs_of(64, 1))
    near = swap(near, "gx", pairs_of(64, 0))
    own = shape(FIELDS * BLOCKS + 2, 8, COLS)
    own_left, own_right, c1, c2, c3 = call(
        interior,
        (own, own) + tuple(shape(FIELDS, count, MEMBERS, COLS) for count in (6, 4, 2)),
        vmem(2),
        [pltpu.VMEM((2, ROWS, 8, COLS), F32)],
        moved=8 * 2**20,
    )(start, geo)
    tile = shape(BLOCKS + 1, 8, COLS)
    outside = shape(FIELDS, 2 * HALO, MEMBERS, COLS)
    halo, wide, left, right, a, b = call(
        strips, (outside, shape(2, EXT, COLS), own, own, tile, tile), vmem(5)
    )(near, far, geo, own_left, own_right)
    b = swap(b, "gy", pairs_of(4, 1))
    a = swap(a, "gy", pairs_of(4, 0))
    rows = pltpu.VMEM((FIELDS, EXT, 8, COLS), F32)
    (last,) = call(
        outer, (outside,), vmem(5), [pltpu.VMEM((2, EXT, 8, COLS), F32), rows, rows], moved=6 * 2**20
    )(start, halo, wide, c1, c2)
    line = pltpu.VMEM((1, OBS), F32)
    edge, part = call(
        observe,
        (shape(FIELDS, BLOCKS, 8, COLS), shape(40, COLS)),
        vmem(7) + hbm(3),
        [pltpu.VMEM((MEMBERS, OBS), F32), pltpu.VMEM((1, OBS), jnp.int32), line, line, dma((3,))],
    )(
        wide, left, right, a, b, c3, last,
        *[
            pltpu.with_memory_space_constraint(value.reshape(1, OBS), pltpu.HBM)
            for value in (obs_cells, obs_values, obs_error)
        ],
    )
    half = shape(FIELDS, ROWS, MEMBERS, COLS, dtype=BF16)
    big, small, mean = call(
        deviate, (half, half, shape(FIELDS * ROWS, COLS)), vmem(3), moved=4 * 2**20
    )(edge, c3, last)
    (out,) = call(
        analyse,
        (shape(*x.shape),),
        vmem(4),
        [pltpu.VMEM(x.shape, F32), dma((FIELDS,))],
        out_specs=tuple(hbm(1)),
    )(summed(part), big, small, mean)
    return out.reshape(FIELDS, MEMBERS, ROWS, COLS)


def solution(mesh):
    placed = (
        P(None, None, "gx", "gy"),
        P("gx", "gy"),
        P("gx", "gy"),
        P("gx", "gy", None),
        P("gx", "gy", None),
        P("gx", "gy", None),
    )
    return jax.shard_map(
        local, mesh=mesh, in_specs=placed, out_specs=P(None, None, "gx", "gy"), check_vma=False
    )
```

```python
import jax
import jax.numpy as jnp
import numpy as np
from jax import lax
from jax.experimental import pallas as pl
from jax.experimental.pallas import tpu as pltpu
from jax.sharding import PartitionSpec as P

F32 = jnp.float32
BF16 = jnp.bfloat16
MEMBERS = 64
BLOCKS = 8
ROWS = 8
COLS = 128
HALO = 3
EXT = ROWS + 2 * HALO
WIDE = 9
OBS = 256
FIELDS = 3
EDGE = FIELDS * HALO * MEMBERS


def vmem(count):
    return [pl.BlockSpec(memory_space=pltpu.VMEM)] * count


def lanes():
    return lax.broadcasted_iota(jnp.int32, (8, COLS), 1)


def grid_sub():
    return lax.broadcasted_iota(jnp.int32, (8, COLS), 0)


def turn(value, shift):
    shift = shift % COLS
    return value if shift == 0 else pltpu.roll(value, shift, 1)


def spread(row):
    return jnp.broadcast_to(row, (8, COLS))


def arrange(x_hbm, depth_hbm, land_hbm, start_ref, geo_ref, near_ref, far_ref, x_ref, depth_ref, land_ref, sems):
    size = MEMBERS * ROWS
    loads = [
        pltpu.make_async_copy(land_hbm, land_ref, sems.at[0]),
        pltpu.make_async_copy(depth_hbm, depth_ref, sems.at[1]),
    ]
    for f in range(FIELDS):
        cut = pl.ds(f * size, size)
        loads.append(pltpu.make_async_copy(x_hbm.at[cut], x_ref.at[cut], sems.at[2 + f]))
    for load in loads:
        load.start()
    odd = lax.rem(lax.axis_index("gx"), 2)
    loads[0].wait()
    loads[1].wait()
    land = land_ref[...].astype(F32)
    geo_ref[0] = 0.125 * depth_ref[...].astype(F32) * land
    geo_ref[1] = land
    low = (ROWS - HALO) * (1 - odd)
    sends = ((near_ref, low), (far_ref, (ROWS - HALO) - low))
    for target, first in sends:
        for g in range(2):
            for r in range(HALO):
                at = EDGE + g * HALO + r
                target[at : at + 1, :] = geo_ref[g, pl.ds(first + r, 1), :]
        target[EDGE + 6 : EDGE + 8, :] = jnp.zeros((2, COLS), F32)
    for f in range(FIELDS):
        loads[2 + f].wait()
        for r in range(ROWS):
            value = x_ref[pl.ds(f * size + r, MEMBERS, stride=ROWS), :]
            start_ref[f, r] = value * land[r : r + 1, :]
        for target, first in sends:
            for r in range(HALO):
                at = (f * HALO + r) * MEMBERS
                target[at : at + MEMBERS, :] = start_ref[f, first + r]


def own_columns(row_of, rows, left, right):
    lane = lanes()
    shifted = lax.rem(lane + HALO, COLS)
    for r in rows:
        value = turn(row_of(r), WIDE * r + HALO)
        left = jnp.where((lane // WIDE == r) & (lax.rem(lane, WIDE) >= HALO), value, left)
        right = jnp.where((shifted // WIDE == r) & (lax.rem(shifted, WIDE) < 2 * HALO), value, right)
    return left, right


def interior(start_ref, geo_ref, left_ref, right_ref, c1_ref, c2_ref, c3_ref, geo):
    for r in range(ROWS):
        geo[0, r] = spread(geo_ref[0, r : r + 1, :])
        geo[1, r] = spread(0.3 * geo_ref[1, r : r + 1, :])
    blank = jnp.zeros((8, COLS), F32)
    inside = range(HALO, HALO + ROWS)

    def block(m, carry):
        at = pl.ds(pl.multiple_of(m * 8, 8), 8)
        for f in range(FIELDS):
            place = f * BLOCKS + m
            left_ref[place], right_ref[place] = own_columns(
                lambda r: start_ref[f, r - HALO, at, :], inside, blank, blank
            )

        def first(f, r):
            return start_ref[f, r, at, :]

        refs = (c1_ref, c2_ref, c3_ref)
        for stage in range(3):
            read = first if stage == 0 else (lambda f, r: refs[stage - 1][f, r - stage, at, :])

            def write(f, r, new):
                refs[stage][f, r - stage - 1, at, :] = new

            advance(stage, range(stage + 1, ROWS - stage - 1), first, read, geo, write)
        return carry

    lax.fori_loop(0, BLOCKS, block, 0)
    for g in range(2):
        place = FIELDS * BLOCKS + g
        left_ref[place], right_ref[place] = own_columns(
            lambda r: spread(geo_ref[g, r - HALO : r - HALO + 1, :]), inside, blank, blank
        )


def strips(near_ref, far_ref, geo_ref, own_left, own_right, halo_ref, wide_ref, left_ref, right_ref, a_ref, b_ref):
    odd_x = lax.rem(lax.axis_index("gx"), 2) == 1
    odd_y = lax.rem(lax.axis_index("gy"), 2) == 1
    field = lax.rem(lanes(), WIDE) // HALO
    outside = tuple(range(HALO)) + tuple(range(HALO + ROWS, EXT))
    place_x = lax.axis_index("gx")
    inside = (place_x > 0) & (place_x < lax.axis_size("gx") - 1)

    def halves(cut):
        near, far = near_ref[cut, :], jnp.where(inside, far_ref[cut, :], 0.0)
        return jnp.where(odd_x, near, far), jnp.where(odd_x, far, near)

    above, below = halves(slice(EDGE, EDGE + 8))
    for g in range(2):
        at = slice(g * HALO, (g + 1) * HALO)
        wide_ref[g, :HALO] = above[at]
        wide_ref[g, HALO : HALO + ROWS] = geo_ref[g]
        wide_ref[g, HALO + ROWS :] = below[at]

    def put(packed, row_of, f, place):
        to_left, to_right = packed
        left, right = own_columns(row_of, outside, own_left[place], own_right[place])
        left_ref[place] = left
        right_ref[place] = right
        to_left = jnp.where(field == f, turn(left, HALO * f - HALO), to_left)
        to_right = jnp.where(field == f, turn(right, HALO * f), to_right)
        return to_left, to_right

    def send(place, packed):
        to_left, to_right = packed
        a_ref[place] = jnp.where(odd_y, to_left, to_right)
        b_ref[place] = jnp.where(odd_y, to_right, to_left)

    def block(m, carry):
        at = pl.ds(pl.multiple_of(m * 8, 8), 8)
        packed = (jnp.zeros((8, COLS), F32),) * 2
        for f in range(FIELDS):
            rows = {}
            for r in range(HALO):
                cut = pl.ds(pl.multiple_of((f * HALO + r) * MEMBERS + m * 8, 8), 8)
                rows[r], rows[r + ROWS + HALO] = halves(cut)
                halo_ref[f, r, at, :] = rows[r]
                halo_ref[f, r + HALO, at, :] = rows[r + ROWS + HALO]
            packed = put(packed, rows.get, f, f * BLOCKS + m)
        send(m, packed)
        return carry

    lax.fori_loop(0, BLOCKS, block, 0, unroll=2)
    packed = (jnp.zeros((8, COLS), F32),) * 2
    for g in range(2):
        packed = put(packed, lambda r: spread(wide_ref[g, r : r + 1, :]), g, FIELDS * BLOCKS + g)
    send(BLOCKS, packed)


def section(h, u, v, depth):
    damp = 0.05 * h
    half = 0.5 * h
    east, north = depth * u, depth * v
    us, vs = 0.05 * u, 0.05 * v
    return dict(
        up=(damp - east, us - half, vs),
        down=(damp + east, us + half, vs),
        back=(damp - north, us, vs - half),
        ahead=(damp + north, us, vs + half),
        here=(-0.2 * h, 0.2 * (v - u), -0.2 * (u + v)),
    )


def tendency(up, down, back, ahead, here):
    return [a + b + c + d + e for a, b, c, d, e in zip(up, down, back, ahead, here)]


def combine(stage, first, old, change):
    new = old + change
    if stage == 0:
        return new
    if stage == 1:
        return 0.75 * first + 0.25 * new
    return (1.0 / 3.0) * first + (2.0 / 3.0) * new


def advance(stage, rows, first, read, geo, write):
    known = {}

    def part_of(r):
        if r not in known:
            known[r] = section(*[read(f, r) for f in range(FIELDS)], geo[0, r])
        return known[r]

    for r in rows:
        mine = part_of(r)
        change = tendency(
            part_of(r + 1)["up"],
            part_of(r - 1)["down"],
            [turn(value, -1) for value in mine["back"]],
            [turn(value, 1) for value in mine["ahead"]],
            mine["here"],
        )
        for f in range(FIELDS):
            write(f, r, combine(stage, first(f, r), read(f, r), geo[1, r] * change[f]))


OUTER = tuple(range(HALO)) + tuple(range(ROWS - HALO, ROWS))


def outer(start_ref, halo_ref, wide_ref, c1_ref, c2_ref, last_ref, geo, s1, s2):
    for r in range(EXT):
        geo[0, r] = spread(wide_ref[0, r : r + 1, :])
        geo[1, r] = spread(0.3 * wide_ref[1, r : r + 1, :])

    def block(m, carry):
        at = pl.ds(pl.multiple_of(m * 8, 8), 8)

        def first(f, r):
            if r < HALO:
                return halo_ref[f, r, at, :]
            if r < HALO + ROWS:
                return start_ref[f, r - HALO, at, :]
            return halo_ref[f, r - ROWS, at, :]

        for stage in range(3):

            def read(f, r):
                if stage == 0:
                    return first(f, r)
                inside = HALO + stage
                if inside <= r < EXT - inside:
                    return (c1_ref, c2_ref)[stage - 1][f, r - inside, at, :]
                return (s1, s2)[stage - 1][f, r]

            def write(f, r, new):
                if stage < 2:
                    (s1, s2)[stage][f, r] = new
                else:
                    last_ref[f, OUTER.index(r - HALO), at, :] = new

            low, high = stage + 1, stage + 1 + HALO
            advance(stage, range(low, high), first, read, geo, write)
            advance(stage, range(EXT - high, EXT - low), first, read, geo, write)
        return carry

    lax.fori_loop(0, BLOCKS, block, 0)


def final_row(f, r, at, inner_ref, outer_ref):
    return outer_ref[f, OUTER.index(r), at, :] if r in OUTER else inner_ref[f, r - HALO, at, :]


def mended(edge, r, value):
    lane = lanes()
    border = (lane < HALO) | (lane >= COLS - HALO)
    return jnp.where(border, turn(edge, -(WIDE * (r + HALO) + HALO)), value)


def observe(
    wide_ref, left_ref, right_ref, a_ref, b_ref, inner_ref, outer_ref, cells_hbm, values_hbm, error_hbm,
    edge_ref, part_ref, seen, cells_ref, values_ref, error_ref, sems,
):
    loads = [
        pltpu.make_async_copy(source, target, sems.at[i])
        for i, (source, target) in enumerate(
            ((cells_hbm, cells_ref), (values_hbm, values_ref), (error_hbm, error_ref))
        )
    ]
    for load in loads:
        load.start()
    place_y = lax.axis_index("gy")
    odd_y = lax.rem(place_y, 2) == 1
    inside = (place_y > 0) & (place_y < lax.axis_size("gy") - 1)
    column = lax.rem(lanes(), WIDE)

    def sides(place, f, own):
        a, b = a_ref[place], jnp.where(inside, b_ref[place], 0.0)
        from_left, from_right = jnp.where(odd_y, a, b), jnp.where(odd_y, b, a)
        left = jnp.where(column < HALO, turn(from_left, -HALO * f), left_ref[own])
        right = jnp.where(
            (column >= HALO) & (column < 2 * HALO), turn(from_right, HALO - HALO * f), right_ref[own]
        )
        return left, right

    depth_sides = sides(BLOCKS, 0, FIELDS * BLOCKS)
    land_sides = [0.3 * value for value in sides(BLOCKS, 1, FIELDS * BLOCKS + 1)]

    def strip(m, carry):
        fields = [sides(m, f, f * BLOCKS + m) for f in range(FIELDS)]
        done = []
        for side in range(2):
            first = [fields[f][side] for f in range(FIELDS)]
            now = first
            for stage in range(3):
                part = section(*now, depth_sides[side])
                change = tendency(
                    [turn(value, -WIDE) for value in part["up"]],
                    [turn(value, WIDE) for value in part["down"]],
                    [turn(value, -1) for value in part["back"]],
                    [turn(value, 1) for value in part["ahead"]],
                    part["here"],
                )
                now = [combine(stage, first[f], now[f], land_sides[side] * change[f]) for f in range(FIELDS)]
            done.append(now)
        for f in range(FIELDS):
            edge_ref[f, m] = jnp.where(column >= HALO, done[0][f], done[1][f])
        return carry

    lax.fori_loop(0, BLOCKS, strip, 0, unroll=4)
    for load in loads:
        load.wait()
    cell = jnp.broadcast_to(cells_ref[...], (8, OBS))
    cell_row, cell_col = cell // COLS, lax.rem(cell, COLS)

    def look(m, carry):
        at = pl.ds(pl.multiple_of(m * 8, 8), 8)
        edge = edge_ref[0, m]
        heights = [mended(edge, r, final_row(0, r, at, inner_ref, outer_ref)) for r in range(ROWS)]
        for part in range(OBS // COLS):
            cut = slice(part * COLS, (part + 1) * COLS)
            got = jnp.zeros((8, COLS), F32)
            for r in range(ROWS):
                picked = jnp.take_along_axis(heights[r], cell_col[:, cut], axis=1)
                got = jnp.where(cell_row[:, cut] == r, picked, got)
            seen[at, cut] = got
        return carry

    lax.fori_loop(0, BLOCKS, look, 0, unroll=4)
    everything = seen[...]
    obs_mean = jnp.sum(everything, axis=0, keepdims=True) * (1.0 / MEMBERS)
    error = error_ref[...]
    scaled = (everything - obs_mean) * (1.0 / (error * np.sqrt(np.float32(MEMBERS - 1))))
    innovation = (values_ref[...] - obs_mean) / error
    product = lax.dot_general(
        jnp.concatenate([scaled, jnp.broadcast_to(innovation, (8, OBS))], axis=0),
        scaled,
        (((1,), (1,)), ((), ())),
        precision=lax.Precision.HIGHEST,
        preferred_element_type=F32,
    )
    half = MEMBERS // 2
    whole = jnp.concatenate([product, jnp.zeros((MEMBERS + 8, COLS - MEMBERS), F32)], axis=1)
    lane, sub = lanes(), grid_sub()
    folded = []
    diagonal = jnp.zeros((8, COLS), F32)
    for k in range(half // 8):
        upper = whole[k * 8 : k * 8 + 8]
        lower = turn(whole[half + k * 8 : half + k * 8 + 8], -half)
        folded.append(jnp.where((lane >= half) | (lane >= sub + 8 * k), upper, lower))
        diagonal = diagonal + jnp.where(lane == sub + 8 * k, lower, 0.0)
    for k in range(2):
        part_ref[k * 8 : k * 8 + 8, :] = jnp.where(lane < MEMBERS, folded[k], turn(folded[k + 2], MEMBERS))
    diagonal = turn(spread(jnp.sum(diagonal, axis=0, keepdims=True)), MEMBERS)
    part_ref[16:, :] = jnp.where(lane < MEMBERS, whole[MEMBERS:], diagonal)


def deviate(edge_ref, inner_ref, outer_ref, big_ref, small_ref, mean_ref):
    for f in range(FIELDS):
        for r in range(ROWS):
            rows = []
            for m in range(BLOCKS):
                at = slice(m * 8, m * 8 + 8)
                rows.append(mended(edge_ref[f, m], r, final_row(f, r, at, inner_ref, outer_ref)))
            value = jnp.concatenate(rows, axis=0)
            mean = jnp.sum(value, axis=0, keepdims=True) * (1.0 / MEMBERS)
            k = f * ROWS + r
            mean_ref[k : k + 1, :] = mean
            value = value - mean
            big = value.astype(BF16)
            big_ref[f, r] = big
            small_ref[f, r] = (value - big.astype(F32)).astype(BF16)


def column_of(value, j):
    return jnp.broadcast_to(value[:, j : j + 1], (8, COLS))


def inverse_factor(sum_ref, flip_ref):
    lane, sub = lanes(), grid_sub()
    half = MEMBERS // 2
    folded = [turn(sum_ref[(k % 2) * 8 : (k % 2) * 8 + 8, :], MEMBERS * (k // 2)) for k in range(4)]
    flip_ref[:, :half] = jnp.transpose(jnp.concatenate(folded, axis=0))
    diagonal = turn(spread(sum_ref[16:17, :]), MEMBERS)
    table = []
    for b in range(BLOCKS):
        k = b % 4
        flipped = flip_ref[k * 8 : k * 8 + 8, :]
        at = sub + 8 * k
        if b < 4:
            value = jnp.where((lane >= at), folded[k], flipped)
        else:
            value = jnp.where(lane < at, folded[k], jnp.where(lane > at, flipped, diagonal))
            value = jnp.where(lane < half, flip_ref[b * 8 : b * 8 + 8, :], turn(value, half))
        one = (lane == sub + 8 * b) | (lane == sub + 8 * b + MEMBERS)
        table.append(jnp.where(lane < MEMBERS, value, 0.0) + jnp.where(one, 1.0, 0.0))
    for b in range(BLOCKS):
        rows = [spread(table[b][s : s + 1, :]) for s in range(8)]
        entry = {(s, t): column_of(rows[s], 8 * b + t) for s in range(8) for t in range(s, 8)}
        over = []
        for s in range(8):
            over.append(1.0 / entry[s, s])
            for t in range(s + 1, 8):
                factor = entry[s, t] * over[s]
                for q in range(t, 8):
                    entry[t, q] = entry[t, q] - factor * entry[s, q]
                rows[t] = rows[t] - factor * rows[s]
        for i in range(b + 1, BLOCKS):
            column = [column_of(table[i], 8 * b + s) for s in range(8)]
            for s in range(8):
                column[s] = column[s] * over[s]
                for t in range(s + 1, 8):
                    column[t] = column[t] - column[s] * entry[s, t]
                table[i] = table[i] - column[s] * rows[s]
        for s in range(8):
            table[b] = jnp.where(sub == s, rows[s] * lax.rsqrt(entry[s, s]), table[b])
    return [jnp.where(lane < MEMBERS, turn(value, MEMBERS), 0.0) for value in table]


def analyse(sum_ref, big_ref, small_ref, mean_ref, out_hbm, out_ref, flip_ref, sems):
    inverse = inverse_factor(sum_ref, flip_ref)
    projection = spread(sum_ref[16:17, :])
    weights = jnp.zeros((8, COLS), F32)
    for b in range(BLOCKS):
        weights = weights + inverse[b] * jnp.sum(inverse[b] * projection, axis=1, keepdims=True)
    weights = jnp.sum(weights, axis=0, keepdims=True) / np.sqrt(np.float32(MEMBERS - 1))
    transform = jnp.concatenate(inverse, axis=0)[:, :MEMBERS] + weights[:, :MEMBERS]
    high = transform.astype(BF16)
    low = (transform - high.astype(F32)).astype(BF16)
    taps = jnp.concatenate([high, low, high], axis=1)
    stores = []
    for f in range(FIELDS):
        for r in range(0, ROWS, 2):
            big = jnp.concatenate([big_ref[f, r], big_ref[f, r + 1]], axis=1)
            small = jnp.concatenate([small_ref[f, r], small_ref[f, r + 1]], axis=1)
            mixed = jnp.dot(taps, jnp.concatenate([big, big, small], axis=0), preferred_element_type=F32)
            for q in range(2):
                k = f * ROWS + r + q
                out_ref[pl.ds(f * MEMBERS * ROWS + r + q, MEMBERS, stride=ROWS), :] = (
                    mean_ref[k : k + 1, :] + mixed[:, q * COLS : (q + 1) * COLS]
                )
        cut = pl.ds(f * MEMBERS * ROWS, MEMBERS * ROWS)
        stores.append(pltpu.make_async_copy(out_ref.at[cut], out_hbm.at[cut], sems.at[f]))
        stores[-1].start()
    for store in stores:
        store.wait()


def swap(value, axis, pairs):
    return lax.ppermute(value, axis, [(a, b) for a, b in pairs] + [(b, a) for a, b in pairs])


def pairs_of(count, first):
    return [(i, (i + 1) % count) for i in range(first, count, 2)]


def summed(part):
    gx, gy = lax.axis_size("gx"), lax.axis_size("gy")
    for flip_x, flip_y in ((1, 0), (1, 1), (1, 3), (17, 0), (49, 0), (3, 0), (5, 0), (13, 0)):
        pairs = [(i * gy + j, (i ^ flip_x) * gy + (j ^ flip_y)) for i in range(gx) for j in range(gy)]
        part = part + lax.ppermute(part, ("gx", "gy"), pairs)
    return part


def shape(*sizes, dtype=F32):
    return jax.ShapeDtypeStruct(sizes, dtype)


def hbm(count):
    return [pl.BlockSpec(memory_space=pltpu.HBM)] * count


def call(body, outs, ins, scratch=(), out_specs=None, moved=2 * 2**20):
    return pl.pallas_call(
        body,
        out_shape=outs,
        in_specs=ins,
        out_specs=out_specs or tuple(vmem(len(outs))),
        scratch_shapes=scratch,
        compiler_params=pltpu.CompilerParams(vmem_limit_bytes=8 * 2**20),
        cost_estimate=pl.CostEstimate(flops=0, transcendentals=0, bytes_accessed=moved),
    )


def local(members_state, depth_level, land_mask, obs_cells, obs_values, obs_error):
    x = members_state.reshape(FIELDS * MEMBERS * ROWS, COLS)
    dma = pltpu.SemaphoreType.DMA
    payload = shape(EDGE + 8, COLS)
    start, geo, near, far = call(
        arrange,
        (shape(FIELDS, ROWS, MEMBERS, COLS), shape(2, ROWS, COLS), payload, payload),
        hbm(3),
        [
            pltpu.VMEM(x.shape, F32), pltpu.VMEM((ROWS, COLS), jnp.int32), pltpu.VMEM((ROWS, COLS), jnp.int32),
            dma((5,)),
        ],
    )(*[pltpu.with_memory_space_constraint(value, pltpu.HBM) for value in (x, depth_level, land_mask)])
    far = swap(far, "gx", pairs_of(64, 1))
    near = swap(near, "gx", pairs_of(64, 0))
    own = shape(FIELDS * BLOCKS + 2, 8, COLS)
    own_left, own_right, c1, c2, c3 = call(
        interior,
        (own, own) + tuple(shape(FIELDS, count, MEMBERS, COLS) for count in (6, 4, 2)),
        vmem(2),
        [pltpu.VMEM((2, ROWS, 8, COLS), F32)],
        moved=8 * 2**20,
    )(start, geo)
    tile = shape(BLOCKS + 1, 8, COLS)
    outside = shape(FIELDS, 2 * HALO, MEMBERS, COLS)
    halo, wide, left, right, a, b = call(
        strips, (outside, shape(2, EXT, COLS), own, own, tile, tile), vmem(5)
    )(near, far, geo, own_left, own_right)
    b = swap(b, "gy", pairs_of(4, 1))
    a = swap(a, "gy", pairs_of(4, 0))
    rows = pltpu.VMEM((FIELDS, EXT, 8, COLS), F32)
    (last,) = call(
        outer, (outside,), vmem(5), [pltpu.VMEM((2, EXT, 8, COLS), F32), rows, rows], moved=6 * 2**20
    )(start, halo, wide, c1, c2)
    line = pltpu.VMEM((1, OBS), F32)
    edge, part = call(
        observe,
        (shape(FIELDS, BLOCKS, 8, COLS), shape(24, COLS)),
        vmem(7) + hbm(3),
        [pltpu.VMEM((MEMBERS, OBS), F32), pltpu.VMEM((1, OBS), jnp.int32), line, line, dma((3,))],
    )(
        wide, left, right, a, b, c3, last,
        *[
            pltpu.with_memory_space_constraint(value.reshape(1, OBS), pltpu.HBM)
            for value in (obs_cells, obs_values, obs_error)
        ],
    )
    half = shape(FIELDS, ROWS, MEMBERS, COLS, dtype=BF16)
    big, small, mean = call(
        deviate, (half, half, shape(FIELDS * ROWS, COLS)), vmem(3), moved=4 * 2**20
    )(edge, c3, last)
    (out,) = call(
        analyse,
        (shape(*x.shape),),
        vmem(4),
        [pltpu.VMEM(x.shape, F32), pltpu.VMEM((COLS, COLS), F32), dma((FIELDS,))],
        out_specs=tuple(hbm(1)),
    )(summed(part), big, small, mean)
    return out.reshape(FIELDS, MEMBERS, ROWS, COLS)


def solution(mesh):
    placed = (
        P(None, None, "gx", "gy"),
        P("gx", "gy"),
        P("gx", "gy"),
        P("gx", "gy", None),
        P("gx", "gy", None),
        P("gx", "gy", None),
    )

    return jax.shard_map(local, mesh=mesh, in_specs=placed, out_specs=P(None, None, "gx", "gy"), check_vma=False)
```

```python
import jax
import jax.numpy as jnp
import numpy as np
from jax import lax
from jax.experimental import pallas as pl
from jax.experimental.pallas import tpu as pltpu
from jax.sharding import PartitionSpec as P

F32 = jnp.float32
BF16 = jnp.bfloat16
MEMBERS = 64
BLOCKS = 8
ROWS = 8
COLS = 128
HALO = 3
EXT = ROWS + 2 * HALO
WIDE = 9
OBS = 256
FIELDS = 3
EDGE = FIELDS * HALO * MEMBERS


def vmem(count):
    return [pl.BlockSpec(memory_space=pltpu.VMEM)] * count


def lanes():
    return lax.broadcasted_iota(jnp.int32, (8, COLS), 1)


def grid_sub():
    return lax.broadcasted_iota(jnp.int32, (8, COLS), 0)


def turn(value, shift):
    shift = shift % COLS
    return value if shift == 0 else pltpu.roll(value, shift, 1)


def spread(row):
    return jnp.broadcast_to(row, (8, COLS))


def arrange(x_hbm, depth_hbm, land_hbm, start_ref, geo_ref, near_ref, far_ref, x_ref, depth_ref, land_ref, sems):
    size = MEMBERS * ROWS
    loads = [
        pltpu.make_async_copy(land_hbm, land_ref, sems.at[0]),
        pltpu.make_async_copy(depth_hbm, depth_ref, sems.at[1]),
    ]
    for f in range(FIELDS):
        cut = pl.ds(f * size, size)
        loads.append(pltpu.make_async_copy(x_hbm.at[cut], x_ref.at[cut], sems.at[2 + f]))
    for load in loads:
        load.start()
    odd = lax.rem(lax.axis_index("gx"), 2)
    loads[0].wait()
    loads[1].wait()
    land = land_ref[...].astype(F32)
    geo_ref[0] = 0.125 * depth_ref[...].astype(F32) * land
    geo_ref[1] = land
    low = (ROWS - HALO) * (1 - odd)
    sends = ((near_ref, low), (far_ref, (ROWS - HALO) - low))
    for target, first in sends:
        for g in range(2):
            for r in range(HALO):
                at = EDGE + g * HALO + r
                target[at : at + 1, :] = geo_ref[g, pl.ds(first + r, 1), :]
        target[EDGE + 6 : EDGE + 8, :] = jnp.zeros((2, COLS), F32)
    for f in range(FIELDS):
        loads[2 + f].wait()
        for r in range(ROWS):
            value = x_ref[pl.ds(f * size + r, MEMBERS, stride=ROWS), :]
            start_ref[f, r] = value * land[r : r + 1, :]
        for target, first in sends:
            for r in range(HALO):
                at = (f * HALO + r) * MEMBERS
                target[at : at + MEMBERS, :] = start_ref[f, first + r]


def own_columns(row_of, rows, left, right):
    lane = lanes()
    shifted = lax.rem(lane + HALO, COLS)
    for r in rows:
        value = turn(row_of(r), WIDE * r + HALO)
        left = jnp.where((lane // WIDE == r) & (lax.rem(lane, WIDE) >= HALO), value, left)
        right = jnp.where((shifted // WIDE == r) & (lax.rem(shifted, WIDE) < 2 * HALO), value, right)
    return left, right


def interior(start_ref, geo_ref, left_ref, right_ref, c1_ref, c2_ref, c3_ref, geo):
    for r in range(ROWS):
        geo[0, r] = spread(geo_ref[0, r : r + 1, :])
        geo[1, r] = spread(0.3 * geo_ref[1, r : r + 1, :])
    blank = jnp.zeros((8, COLS), F32)
    inside = range(HALO, HALO + ROWS)

    def block(m, carry):
        at = pl.ds(pl.multiple_of(m * 8, 8), 8)
        for f in range(FIELDS):
            place = f * BLOCKS + m
            left_ref[place], right_ref[place] = own_columns(
                lambda r: start_ref[f, r - HALO, at, :], inside, blank, blank
            )

        def first(f, r):
            return start_ref[f, r, at, :]

        refs = (c1_ref, c2_ref, c3_ref)
        for stage in range(3):
            read = first if stage == 0 else (lambda f, r: refs[stage - 1][f, r - stage, at, :])

            def write(f, r, new):
                refs[stage][f, r - stage - 1, at, :] = new

            advance(stage, range(stage + 1, ROWS - stage - 1), first, read, geo, write)
        return carry

    lax.fori_loop(0, BLOCKS, block, 0)
    for g in range(2):
        place = FIELDS * BLOCKS + g
        left_ref[place], right_ref[place] = own_columns(
            lambda r: spread(geo_ref[g, r - HALO : r - HALO + 1, :]), inside, blank, blank
        )


def strips(near_ref, far_ref, geo_ref, own_left, own_right, halo_ref, wide_ref, left_ref, right_ref, a_ref, b_ref):
    odd_x = lax.rem(lax.axis_index("gx"), 2) == 1
    odd_y = lax.rem(lax.axis_index("gy"), 2) == 1
    field = lax.rem(lanes(), WIDE) // HALO
    outside = tuple(range(HALO)) + tuple(range(HALO + ROWS, EXT))

    def halves(cut):
        near, far = near_ref[cut, :], far_ref[cut, :]
        return jnp.where(odd_x, near, far), jnp.where(odd_x, far, near)

    above, below = halves(slice(EDGE, EDGE + 8))
    for g in range(2):
        at = slice(g * HALO, (g + 1) * HALO)
        wide_ref[g, :HALO] = above[at]
        wide_ref[g, HALO : HALO + ROWS] = geo_ref[g]
        wide_ref[g, HALO + ROWS :] = below[at]

    def put(packed, row_of, f, place):
        to_left, to_right = packed
        left, right = own_columns(row_of, outside, own_left[place], own_right[place])
        left_ref[place] = left
        right_ref[place] = right
        to_left = jnp.where(field == f, turn(left, HALO * f - HALO), to_left)
        to_right = jnp.where(field == f, turn(right, HALO * f), to_right)
        return to_left, to_right

    def send(place, packed):
        to_left, to_right = packed
        a_ref[place] = jnp.where(odd_y, to_left, to_right)
        b_ref[place] = jnp.where(odd_y, to_right, to_left)

    def block(m, carry):
        at = pl.ds(pl.multiple_of(m * 8, 8), 8)
        packed = (jnp.zeros((8, COLS), F32),) * 2
        for f in range(FIELDS):
            rows = {}
            for r in range(HALO):
                cut = pl.ds(pl.multiple_of((f * HALO + r) * MEMBERS + m * 8, 8), 8)
                rows[r], rows[r + ROWS + HALO] = halves(cut)
                halo_ref[f, r, at, :] = rows[r]
                halo_ref[f, r + HALO, at, :] = rows[r + ROWS + HALO]
            packed = put(packed, rows.get, f, f * BLOCKS + m)
        send(m, packed)
        return carry

    lax.fori_loop(0, BLOCKS, block, 0, unroll=2)
    packed = (jnp.zeros((8, COLS), F32),) * 2
    for g in range(2):
        packed = put(packed, lambda r: spread(wide_ref[g, r : r + 1, :]), g, FIELDS * BLOCKS + g)
    send(BLOCKS, packed)


def section(h, u, v, depth):
    damp = 0.05 * h
    half = 0.5 * h
    east, north = depth * u, depth * v
    us, vs = 0.05 * u, 0.05 * v
    return dict(
        up=(damp - east, us - half, vs),
        down=(damp + east, us + half, vs),
        back=(damp - north, us, vs - half),
        ahead=(damp + north, us, vs + half),
        here=(-0.2 * h, 0.2 * (v - u), -0.2 * (u + v)),
    )


def tendency(up, down, back, ahead, here):
    return [a + b + c + d + e for a, b, c, d, e in zip(up, down, back, ahead, here)]


def combine(stage, first, old, change):
    new = old + change
    if stage == 0:
        return new
    if stage == 1:
        return 0.75 * first + 0.25 * new
    return (1.0 / 3.0) * first + (2.0 / 3.0) * new


def advance(stage, rows, first, read, geo, write):
    known = {}

    def part_of(r):
        if r not in known:
            known[r] = section(*[read(f, r) for f in range(FIELDS)], geo[0, r])
        return known[r]

    for r in rows:
        mine = part_of(r)
        change = tendency(
            part_of(r + 1)["up"],
            part_of(r - 1)["down"],
            [turn(value, -1) for value in mine["back"]],
            [turn(value, 1) for value in mine["ahead"]],
            mine["here"],
        )
        for f in range(FIELDS):
            write(f, r, combine(stage, first(f, r), read(f, r), geo[1, r] * change[f]))


OUTER = tuple(range(HALO)) + tuple(range(ROWS - HALO, ROWS))


def outer(
    start_ref, halo_ref, wide_ref, c1_ref, c2_ref, cells_hbm, values_hbm, error_hbm,
    last_ref, cell_ref, weight_ref, geo, s1, s2, cells_ref, values_ref, error_ref, sems,
):
    loads = [
        pltpu.make_async_copy(source, target, sems.at[i])
        for i, (source, target) in enumerate(
            ((cells_hbm, cells_ref), (values_hbm, values_ref), (error_hbm, error_ref))
        )
    ]
    for load in loads:
        load.start()
    for r in range(EXT):
        geo[0, r] = spread(wide_ref[0, r : r + 1, :])
        geo[1, r] = spread(0.3 * wide_ref[1, r : r + 1, :])

    def block(m, carry):
        at = pl.ds(pl.multiple_of(m * 8, 8), 8)

        def first(f, r):
            if r < HALO:
                return halo_ref[f, r, at, :]
            if r < HALO + ROWS:
                return start_ref[f, r - HALO, at, :]
            return halo_ref[f, r - ROWS, at, :]

        for stage in range(3):

            def read(f, r):
                if stage == 0:
                    return first(f, r)
                inside = HALO + stage
                if inside <= r < EXT - inside:
                    return (c1_ref, c2_ref)[stage - 1][f, r - inside, at, :]
                return (s1, s2)[stage - 1][f, r]

            def write(f, r, new):
                if stage < 2:
                    (s1, s2)[stage][f, r] = new
                else:
                    last_ref[f, OUTER.index(r - HALO), at, :] = new

            low, high = stage + 1, stage + 1 + HALO
            advance(stage, range(low, high), first, read, geo, write)
            advance(stage, range(EXT - high, EXT - low), first, read, geo, write)
        return carry

    lax.fori_loop(0, BLOCKS, block, 0)
    for load in loads:
        load.wait()
    cell = jnp.broadcast_to(cells_ref[...], (8, OBS))
    cell_ref[0] = cell // COLS
    cell_ref[1] = lax.rem(cell, COLS)
    error = error_ref[...]
    weight_ref[0:1, :] = 1.0 / (error * np.sqrt(np.float32(MEMBERS - 1)))
    weight_ref[1:2, :] = 1.0 / error
    weight_ref[2:3, :] = values_ref[...]


def final_row(f, r, at, inner_ref, outer_ref):
    return outer_ref[f, OUTER.index(r), at, :] if r in OUTER else inner_ref[f, r - HALO, at, :]


def mended(edge, r, value):
    lane = lanes()
    border = (lane < HALO) | (lane >= COLS - HALO)
    return jnp.where(border, turn(edge, -(WIDE * (r + HALO) + HALO)), value)


def observe(
    left_ref, right_ref, a_ref, b_ref, inner_ref, outer_ref, cell_ref, weight_ref, edge_ref, part_ref, seen
):
    place_y = lax.axis_index("gy")
    odd_y = lax.rem(place_y, 2) == 1
    inside = (place_y > 0) & (place_y < lax.axis_size("gy") - 1)
    column = lax.rem(lanes(), WIDE)

    def sides(place, f, own):
        a, b = a_ref[place], jnp.where(inside, b_ref[place], 0.0)
        from_left, from_right = jnp.where(odd_y, a, b), jnp.where(odd_y, b, a)
        left = jnp.where(column < HALO, turn(from_left, -HALO * f), left_ref[own])
        right = jnp.where(
            (column >= HALO) & (column < 2 * HALO), turn(from_right, HALO - HALO * f), right_ref[own]
        )
        return left, right

    depth_sides = sides(BLOCKS, 0, FIELDS * BLOCKS)
    land_sides = [0.3 * value for value in sides(BLOCKS, 1, FIELDS * BLOCKS + 1)]

    cell_row, cell_col = cell_ref[0], cell_ref[1]

    def strip(m, carry):
        fields = [sides(m, f, f * BLOCKS + m) for f in range(FIELDS)]
        done = []
        for side in range(2):
            first = [fields[f][side] for f in range(FIELDS)]
            now = first
            for stage in range(3):
                part = section(*now, depth_sides[side])
                change = tendency(
                    [turn(value, -WIDE) for value in part["up"]],
                    [turn(value, WIDE) for value in part["down"]],
                    [turn(value, -1) for value in part["back"]],
                    [turn(value, 1) for value in part["ahead"]],
                    part["here"],
                )
                now = [combine(stage, first[f], now[f], land_sides[side] * change[f]) for f in range(FIELDS)]
            done.append(now)
        edges = [jnp.where(column >= HALO, done[0][f], done[1][f]) for f in range(FIELDS)]
        for f in range(FIELDS):
            edge_ref[f, m] = edges[f]
        at = pl.ds(pl.multiple_of(m * 8, 8), 8)
        heights = [mended(edges[0], r, final_row(0, r, at, inner_ref, outer_ref)) for r in range(ROWS)]
        for part in range(OBS // COLS):
            cut = slice(part * COLS, (part + 1) * COLS)
            got = jnp.zeros((8, COLS), F32)
            for r in range(ROWS):
                picked = jnp.take_along_axis(heights[r], cell_col[:, cut], axis=1)
                got = jnp.where(cell_row[:, cut] == r, picked, got)
            seen[at, cut] = got
        return carry

    lax.fori_loop(0, BLOCKS, strip, 0, unroll=4)
    everything = seen[...]
    obs_mean = jnp.sum(everything, axis=0, keepdims=True) * (1.0 / MEMBERS)
    scaled = (everything - obs_mean) * weight_ref[0:1, :]
    innovation = (weight_ref[2:3, :] - obs_mean) * weight_ref[1:2, :]
    product = lax.dot_general(
        jnp.concatenate([scaled, jnp.broadcast_to(innovation, (8, OBS))], axis=0),
        scaled,
        (((1,), (1,)), ((), ())),
        precision=lax.Precision.HIGHEST,
        preferred_element_type=F32,
    )
    half = MEMBERS // 2
    whole = jnp.concatenate([product, jnp.zeros((MEMBERS + 8, COLS - MEMBERS), F32)], axis=1)
    lane, sub = lanes(), grid_sub()
    folded = []
    diagonal = jnp.zeros((8, COLS), F32)
    for k in range(half // 8):
        upper = whole[k * 8 : k * 8 + 8]
        lower = turn(whole[half + k * 8 : half + k * 8 + 8], -half)
        folded.append(jnp.where((lane >= half) | (lane >= sub + 8 * k), upper, lower))
        diagonal = diagonal + jnp.where(lane == sub + 8 * k, lower, 0.0)
    for k in range(2):
        part_ref[k * 8 : k * 8 + 8, :] = jnp.where(lane < MEMBERS, folded[k], turn(folded[k + 2], MEMBERS))
    diagonal = turn(spread(jnp.sum(diagonal, axis=0, keepdims=True)), MEMBERS)
    part_ref[16:, :] = jnp.where(lane < MEMBERS, whole[MEMBERS:], diagonal)


def deviate(edge_ref, inner_ref, outer_ref, big_ref, small_ref, mean_ref):
    for f in range(FIELDS):
        for r in range(ROWS):
            rows = []
            for m in range(BLOCKS):
                at = slice(m * 8, m * 8 + 8)
                rows.append(mended(edge_ref[f, m], r, final_row(f, r, at, inner_ref, outer_ref)))
            value = jnp.concatenate(rows, axis=0)
            mean = jnp.sum(value, axis=0, keepdims=True) * (1.0 / MEMBERS)
            k = f * ROWS + r
            mean_ref[k : k + 1, :] = mean
            value = value - mean
            big = value.astype(BF16)
            big_ref[f, r] = big
            small_ref[f, r] = (value - big.astype(F32)).astype(BF16)


def column_of(value, j):
    return jnp.broadcast_to(value[:, j : j + 1], (8, COLS))


def inverse_factor(sum_ref, flip_ref):
    lane, sub = lanes(), grid_sub()
    half = MEMBERS // 2
    folded = [turn(sum_ref[(k % 2) * 8 : (k % 2) * 8 + 8, :], MEMBERS * (k // 2)) for k in range(4)]
    flip_ref[:, :half] = jnp.transpose(jnp.concatenate(folded, axis=0))
    diagonal = turn(spread(sum_ref[16:17, :]), MEMBERS)
    table = []
    for b in range(BLOCKS):
        k = b % 4
        flipped = flip_ref[k * 8 : k * 8 + 8, :]
        at = sub + 8 * k
        if b < 4:
            value = jnp.where((lane >= at), folded[k], flipped)
        else:
            value = jnp.where(lane < at, folded[k], jnp.where(lane > at, flipped, diagonal))
            value = jnp.where(lane < half, flip_ref[b * 8 : b * 8 + 8, :], turn(value, half))
        one = (lane == sub + 8 * b) | (lane == sub + 8 * b + MEMBERS)
        table.append(jnp.where(lane < MEMBERS, value, 0.0) + jnp.where(one, 1.0, 0.0))
    for b in range(BLOCKS):
        rows = [spread(table[b][s : s + 1, :]) for s in range(8)]
        entry = {(s, t): column_of(rows[s], 8 * b + t) for s in range(8) for t in range(s, 8)}
        over = []
        for s in range(8):
            over.append(1.0 / entry[s, s])
            for t in range(s + 1, 8):
                factor = entry[s, t] * over[s]
                for q in range(t, 8):
                    entry[t, q] = entry[t, q] - factor * entry[s, q]
                rows[t] = rows[t] - factor * rows[s]
        for i in range(b + 1, BLOCKS):
            column = [column_of(table[i], 8 * b + s) for s in range(8)]
            for s in range(8):
                column[s] = column[s] * over[s]
                for t in range(s + 1, 8):
                    column[t] = column[t] - column[s] * entry[s, t]
                table[i] = table[i] - column[s] * rows[s]
        for s in range(8):
            table[b] = jnp.where(sub == s, rows[s] * lax.rsqrt(entry[s, s]), table[b])
    return [jnp.where(lane < MEMBERS, turn(value, MEMBERS), 0.0) for value in table]


def analyse(sum_ref, big_ref, small_ref, mean_ref, out_hbm, out_ref, flip_ref, sems):
    inverse = inverse_factor(sum_ref, flip_ref)
    projection = spread(sum_ref[16:17, :])
    weights = jnp.zeros((8, COLS), F32)
    for b in range(BLOCKS):
        weights = weights + inverse[b] * jnp.sum(inverse[b] * projection, axis=1, keepdims=True)
    weights = jnp.sum(weights, axis=0, keepdims=True) / np.sqrt(np.float32(MEMBERS - 1))
    transform = jnp.concatenate(inverse, axis=0)[:, :MEMBERS] + weights[:, :MEMBERS]
    high = transform.astype(BF16)
    low = (transform - high.astype(F32)).astype(BF16)
    taps = jnp.concatenate([high, low, high], axis=1)
    stores = []
    for f in range(FIELDS):
        for r in range(0, ROWS, 2):
            big = jnp.concatenate([big_ref[f, r], big_ref[f, r + 1]], axis=1)
            small = jnp.concatenate([small_ref[f, r], small_ref[f, r + 1]], axis=1)
            mixed = jnp.dot(taps, jnp.concatenate([big, big, small], axis=0), preferred_element_type=F32)
            for q in range(2):
                k = f * ROWS + r + q
                out_ref[pl.ds(f * MEMBERS * ROWS + r + q, MEMBERS, stride=ROWS), :] = (
                    mean_ref[k : k + 1, :] + mixed[:, q * COLS : (q + 1) * COLS]
                )
        cut = pl.ds(f * MEMBERS * ROWS, MEMBERS * ROWS)
        stores.append(pltpu.make_async_copy(out_ref.at[cut], out_hbm.at[cut], sems.at[f]))
        stores[-1].start()
    for store in stores:
        store.wait()


def swap(value, axis, pairs):
    return lax.ppermute(value, axis, [(a, b) for a, b in pairs] + [(b, a) for a, b in pairs])


def pairs_of(count, first, wrap=False):
    return [(i, (i + 1) % count) for i in range(first, count if wrap else count - 1, 2)]


def summed(part):
    gx, gy = lax.axis_size("gx"), lax.axis_size("gy")
    for flip_x, flip_y in ((1, 0), (1, 1), (1, 3), (17, 0), (49, 0), (3, 0), (5, 0), (13, 0)):
        pairs = [(i * gy + j, (i ^ flip_x) * gy + (j ^ flip_y)) for i in range(gx) for j in range(gy)]
        part = part + lax.ppermute(part, ("gx", "gy"), pairs)
    return part


def shape(*sizes, dtype=F32):
    return jax.ShapeDtypeStruct(sizes, dtype)


def hbm(count):
    return [pl.BlockSpec(memory_space=pltpu.HBM)] * count


def call(body, outs, ins, scratch=(), out_specs=None, moved=2 * 2**20):
    return pl.pallas_call(
        body,
        out_shape=outs,
        in_specs=ins,
        out_specs=out_specs or tuple(vmem(len(outs))),
        scratch_shapes=scratch,
        compiler_params=pltpu.CompilerParams(vmem_limit_bytes=8 * 2**20),
        cost_estimate=pl.CostEstimate(flops=0, transcendentals=0, bytes_accessed=moved),
    )


def local(members_state, depth_level, land_mask, obs_cells, obs_values, obs_error):
    x = members_state.reshape(FIELDS * MEMBERS * ROWS, COLS)
    dma = pltpu.SemaphoreType.DMA
    payload = shape(EDGE + 8, COLS)
    start, geo, near, far = call(
        arrange,
        (shape(FIELDS, ROWS, MEMBERS, COLS), shape(2, ROWS, COLS), payload, payload),
        hbm(3),
        [
            pltpu.VMEM(x.shape, F32), pltpu.VMEM((ROWS, COLS), jnp.int32), pltpu.VMEM((ROWS, COLS), jnp.int32),
            dma((5,)),
        ],
    )(*[pltpu.with_memory_space_constraint(value, pltpu.HBM) for value in (x, depth_level, land_mask)])
    far = swap(far, "gx", pairs_of(64, 1))
    near = swap(near, "gx", pairs_of(64, 0))
    own = shape(FIELDS * BLOCKS + 2, 8, COLS)
    own_left, own_right, c1, c2, c3 = call(
        interior,
        (own, own) + tuple(shape(FIELDS, count, MEMBERS, COLS) for count in (6, 4, 2)),
        vmem(2),
        [pltpu.VMEM((2, ROWS, 8, COLS), F32)],
        moved=8 * 2**20,
    )(start, geo)
    tile = shape(BLOCKS + 1, 8, COLS)
    outside = shape(FIELDS, 2 * HALO, MEMBERS, COLS)
    halo, wide, left, right, a, b = call(
        strips, (outside, shape(2, EXT, COLS), own, own, tile, tile), vmem(5)
    )(near, far, geo, own_left, own_right)
    b = swap(b, "gy", pairs_of(4, 1, wrap=True))
    a = swap(a, "gy", pairs_of(4, 0))
    rows = pltpu.VMEM((FIELDS, EXT, 8, COLS), F32)
    line = pltpu.VMEM((1, OBS), F32)
    last, cell, weight = call(
        outer,
        (outside, jax.ShapeDtypeStruct((2, 8, OBS), jnp.int32), shape(8, OBS)),
        vmem(5) + hbm(3),
        [
            pltpu.VMEM((2, EXT, 8, COLS), F32), rows, rows,
            pltpu.VMEM((1, OBS), jnp.int32), line, line, dma((3,)),
        ],
        moved=6 * 2**20,
    )(
        start, halo, wide, c1, c2,
        *[
            pltpu.with_memory_space_constraint(value.reshape(1, OBS), pltpu.HBM)
            for value in (obs_cells, obs_values, obs_error)
        ],
    )
    edge, part = call(
        observe,
        (shape(FIELDS, BLOCKS, 8, COLS), shape(24, COLS)),
        vmem(8),
        [pltpu.VMEM((MEMBERS, OBS), F32)],
    )(left, right, a, b, c3, last, cell, weight)
    half = shape(FIELDS, ROWS, MEMBERS, COLS, dtype=BF16)
    big, small, mean = call(
        deviate, (half, half, shape(FIELDS * ROWS, COLS)), vmem(3), moved=4 * 2**20
    )(edge, c3, last)
    (out,) = call(
        analyse,
        (shape(*x.shape),),
        vmem(4),
        [pltpu.VMEM(x.shape, F32), pltpu.VMEM((COLS, COLS), F32), dma((FIELDS,))],
        out_specs=tuple(hbm(1)),
    )(summed(part), big, small, mean)
    return out.reshape(FIELDS, MEMBERS, ROWS, COLS)


def solution(mesh):
    placed = (
        P(None, None, "gx", "gy"),
        P("gx", "gy"),
        P("gx", "gy"),
        P("gx", "gy", None),
        P("gx", "gy", None),
        P("gx", "gy", None),
    )

    return jax.shard_map(local, mesh=mesh, in_specs=placed, out_specs=P(None, None, "gx", "gy"), check_vma=False)
```

```python
import jax
import jax.numpy as jnp
import numpy as np
from jax import lax
from jax.experimental import pallas as pl
from jax.experimental.pallas import tpu as pltpu
from jax.sharding import PartitionSpec as P

F32 = jnp.float32
BF16 = jnp.bfloat16
MEMBERS = 64
BLOCKS = 8
ROWS = 8
COLS = 128
HALO = 3
EXT = ROWS + 2 * HALO
WIDE = 9
OBS = 256
FIELDS = 3
EDGE = FIELDS * HALO * MEMBERS


def vmem(count):
    return [pl.BlockSpec(memory_space=pltpu.VMEM)] * count


def lanes():
    return lax.broadcasted_iota(jnp.int32, (8, COLS), 1)


def grid_sub():
    return lax.broadcasted_iota(jnp.int32, (8, COLS), 0)


def turn(value, shift):
    shift = shift % COLS
    return value if shift == 0 else pltpu.roll(value, shift, 1)


def spread(row):
    return jnp.broadcast_to(row, (8, COLS))


def arrange(x_hbm, depth_hbm, land_hbm, start_ref, geo_ref, near_ref, far_ref, x_ref, depth_ref, land_ref, sems):
    size = MEMBERS * ROWS
    loads = [
        pltpu.make_async_copy(land_hbm, land_ref, sems.at[0]),
        pltpu.make_async_copy(depth_hbm, depth_ref, sems.at[1]),
    ]
    for f in range(FIELDS):
        cut = pl.ds(f * size, size)
        loads.append(pltpu.make_async_copy(x_hbm.at[cut], x_ref.at[cut], sems.at[2 + f]))
    for load in loads:
        load.start()
    odd = lax.rem(lax.axis_index("gx"), 2)
    loads[0].wait()
    loads[1].wait()
    land = land_ref[...].astype(F32)
    geo_ref[0] = 0.125 * depth_ref[...].astype(F32) * land
    geo_ref[1] = land
    low = (ROWS - HALO) * (1 - odd)
    sends = ((near_ref, low), (far_ref, (ROWS - HALO) - low))
    for target, first in sends:
        for g in range(2):
            for r in range(HALO):
                at = EDGE + g * HALO + r
                target[at : at + 1, :] = geo_ref[g, pl.ds(first + r, 1), :]
        target[EDGE + 6 : EDGE + 8, :] = jnp.zeros((2, COLS), F32)
    for f in range(FIELDS):
        loads[2 + f].wait()
        for r in range(ROWS):
            value = x_ref[pl.ds(f * size + r, MEMBERS, stride=ROWS), :]
            start_ref[f, r] = value * land[r : r + 1, :]
        for target, first in sends:
            for r in range(HALO):
                at = (f * HALO + r) * MEMBERS
                target[at : at + MEMBERS, :] = start_ref[f, first + r]


def own_columns(row_of, rows, left, right):
    lane = lanes()
    shifted = lax.rem(lane + HALO, COLS)
    for r in rows:
        value = turn(row_of(r), WIDE * r + HALO)
        left = jnp.where((lane // WIDE == r) & (lax.rem(lane, WIDE) >= HALO), value, left)
        right = jnp.where((shifted // WIDE == r) & (lax.rem(shifted, WIDE) < 2 * HALO), value, right)
    return left, right


def interior(start_ref, geo_ref, left_ref, right_ref, c1_ref, c2_ref, c3_ref, geo):
    for r in range(ROWS):
        geo[0, r] = spread(geo_ref[0, r : r + 1, :])
        geo[1, r] = spread(0.3 * geo_ref[1, r : r + 1, :])
    blank = jnp.zeros((8, COLS), F32)
    inside = range(HALO, HALO + ROWS)

    def block(m, carry):
        at = pl.ds(pl.multiple_of(m * 8, 8), 8)
        for f in range(FIELDS):
            place = f * BLOCKS + m
            left_ref[place], right_ref[place] = own_columns(
                lambda r: start_ref[f, r - HALO, at, :], inside, blank, blank
            )

        def first(f, r):
            return start_ref[f, r, at, :]

        refs = (c1_ref, c2_ref, c3_ref)
        for stage in range(3):
            read = first if stage == 0 else (lambda f, r: refs[stage - 1][f, r - stage, at, :])

            def write(f, r, new):
                refs[stage][f, r - stage - 1, at, :] = new

            advance(stage, range(stage + 1, ROWS - stage - 1), first, read, geo, write)
        return carry

    lax.fori_loop(0, BLOCKS, block, 0)
    for g in range(2):
        place = FIELDS * BLOCKS + g
        left_ref[place], right_ref[place] = own_columns(
            lambda r: spread(geo_ref[g, r - HALO : r - HALO + 1, :]), inside, blank, blank
        )


def strips(near_ref, far_ref, geo_ref, own_left, own_right, halo_ref, wide_ref, left_ref, right_ref, a_ref, b_ref):
    odd_x = lax.rem(lax.axis_index("gx"), 2) == 1
    odd_y = lax.rem(lax.axis_index("gy"), 2) == 1
    field = lax.rem(lanes(), WIDE) // HALO
    outside = tuple(range(HALO)) + tuple(range(HALO + ROWS, EXT))

    def halves(cut):
        near, far = near_ref[cut, :], far_ref[cut, :]
        return jnp.where(odd_x, near, far), jnp.where(odd_x, far, near)

    above, below = halves(slice(EDGE, EDGE + 8))
    for g in range(2):
        at = slice(g * HALO, (g + 1) * HALO)
        wide_ref[g, :HALO] = above[at]
        wide_ref[g, HALO : HALO + ROWS] = geo_ref[g]
        wide_ref[g, HALO + ROWS :] = below[at]

    def put(packed, row_of, f, place):
        to_left, to_right = packed
        left, right = own_columns(row_of, outside, own_left[place], own_right[place])
        left_ref[place] = left
        right_ref[place] = right
        to_left = jnp.where(field == f, turn(left, HALO * f - HALO), to_left)
        to_right = jnp.where(field == f, turn(right, HALO * f), to_right)
        return to_left, to_right

    def send(place, packed):
        to_left, to_right = packed
        a_ref[place] = jnp.where(odd_y, to_left, to_right)
        b_ref[place] = jnp.where(odd_y, to_right, to_left)

    def block(m, carry):
        at = pl.ds(pl.multiple_of(m * 8, 8), 8)
        packed = (jnp.zeros((8, COLS), F32),) * 2
        for f in range(FIELDS):
            rows = {}
            for r in range(HALO):
                cut = pl.ds(pl.multiple_of((f * HALO + r) * MEMBERS + m * 8, 8), 8)
                rows[r], rows[r + ROWS + HALO] = halves(cut)
                halo_ref[f, r, at, :] = rows[r]
                halo_ref[f, r + HALO, at, :] = rows[r + ROWS + HALO]
            packed = put(packed, rows.get, f, f * BLOCKS + m)
        send(m, packed)
        return carry

    lax.fori_loop(0, BLOCKS, block, 0, unroll=4)
    packed = (jnp.zeros((8, COLS), F32),) * 2
    for g in range(2):
        packed = put(packed, lambda r: spread(wide_ref[g, r : r + 1, :]), g, FIELDS * BLOCKS + g)
    send(BLOCKS, packed)


def section(h, u, v, depth):
    damp = 0.05 * h
    half = 0.5 * h
    east, north = depth * u, depth * v
    us, vs = 0.05 * u, 0.05 * v
    return dict(
        up=(damp - east, us - half, vs),
        down=(damp + east, us + half, vs),
        back=(damp - north, us, vs - half),
        ahead=(damp + north, us, vs + half),
        here=(-0.2 * h, 0.2 * (v - u), -0.2 * (u + v)),
    )


def tendency(up, down, back, ahead, here):
    return [a + b + c + d + e for a, b, c, d, e in zip(up, down, back, ahead, here)]


def combine(stage, first, old, change):
    new = old + change
    if stage == 0:
        return new
    if stage == 1:
        return 0.75 * first + 0.25 * new
    return (1.0 / 3.0) * first + (2.0 / 3.0) * new


def advance(stage, rows, first, read, geo, write):
    known = {}

    def part_of(r):
        if r not in known:
            known[r] = section(*[read(f, r) for f in range(FIELDS)], geo[0, r])
        return known[r]

    for r in rows:
        mine = part_of(r)
        change = tendency(
            part_of(r + 1)["up"],
            part_of(r - 1)["down"],
            [turn(value, -1) for value in mine["back"]],
            [turn(value, 1) for value in mine["ahead"]],
            mine["here"],
        )
        for f in range(FIELDS):
            write(f, r, combine(stage, first(f, r), read(f, r), geo[1, r] * change[f]))


OUTER = tuple(range(HALO)) + tuple(range(ROWS - HALO, ROWS))


def outer(
    start_ref, halo_ref, wide_ref, c1_ref, c2_ref, cells_hbm, values_hbm, error_hbm,
    last_ref, cell_ref, weight_ref, geo, s1, s2, cells_ref, values_ref, error_ref, sems,
):
    loads = [
        pltpu.make_async_copy(source, target, sems.at[i])
        for i, (source, target) in enumerate(
            ((cells_hbm, cells_ref), (values_hbm, values_ref), (error_hbm, error_ref))
        )
    ]
    for load in loads:
        load.start()
    for r in range(EXT):
        geo[0, r] = spread(wide_ref[0, r : r + 1, :])
        geo[1, r] = spread(0.3 * wide_ref[1, r : r + 1, :])

    def block(m, carry):
        at = pl.ds(pl.multiple_of(m * 8, 8), 8)

        def first(f, r):
            if r < HALO:
                return halo_ref[f, r, at, :]
            if r < HALO + ROWS:
                return start_ref[f, r - HALO, at, :]
            return halo_ref[f, r - ROWS, at, :]

        for stage in range(3):

            def read(f, r):
                if stage == 0:
                    return first(f, r)
                inside = HALO + stage
                if inside <= r < EXT - inside:
                    return (c1_ref, c2_ref)[stage - 1][f, r - inside, at, :]
                return (s1, s2)[stage - 1][f, r]

            def write(f, r, new):
                if stage < 2:
                    (s1, s2)[stage][f, r] = new
                else:
                    last_ref[f, OUTER.index(r - HALO), at, :] = new

            low, high = stage + 1, stage + 1 + HALO
            advance(stage, range(low, high), first, read, geo, write)
            advance(stage, range(EXT - high, EXT - low), first, read, geo, write)
        return carry

    lax.fori_loop(0, BLOCKS, block, 0)
    for load in loads:
        load.wait()
    cell = jnp.broadcast_to(cells_ref[...], (8, OBS))
    cell_ref[0] = cell // COLS
    cell_ref[1] = lax.rem(cell, COLS)
    error = error_ref[...]
    weight_ref[0:1, :] = 1.0 / (error * np.sqrt(np.float32(MEMBERS - 1)))
    weight_ref[1:2, :] = 1.0 / error
    weight_ref[2:3, :] = values_ref[...]


def final_row(f, r, at, inner_ref, outer_ref):
    return outer_ref[f, OUTER.index(r), at, :] if r in OUTER else inner_ref[f, r - HALO, at, :]


def mended(edge, r, value):
    lane = lanes()
    border = (lane < HALO) | (lane >= COLS - HALO)
    return jnp.where(border, turn(edge, -(WIDE * (r + HALO) + HALO)), value)


def observe(
    left_ref, right_ref, a_ref, b_ref, inner_ref, outer_ref, cell_ref, weight_ref, edge_ref, part_ref, seen
):
    place_y = lax.axis_index("gy")
    odd_y = lax.rem(place_y, 2) == 1
    inside = (place_y > 0) & (place_y < lax.axis_size("gy") - 1)
    column = lax.rem(lanes(), WIDE)

    def sides(place, f, own):
        a, b = a_ref[place], jnp.where(inside, b_ref[place], 0.0)
        from_left, from_right = jnp.where(odd_y, a, b), jnp.where(odd_y, b, a)
        left = jnp.where(column < HALO, turn(from_left, -HALO * f), left_ref[own])
        right = jnp.where(
            (column >= HALO) & (column < 2 * HALO), turn(from_right, HALO - HALO * f), right_ref[own]
        )
        return left, right

    depth_sides = sides(BLOCKS, 0, FIELDS * BLOCKS)
    land_sides = [0.3 * value for value in sides(BLOCKS, 1, FIELDS * BLOCKS + 1)]

    cell_row, cell_col = cell_ref[0], cell_ref[1]

    def strip(m, carry):
        fields = [sides(m, f, f * BLOCKS + m) for f in range(FIELDS)]
        done = []
        for side in range(2):
            first = [fields[f][side] for f in range(FIELDS)]
            now = first
            for stage in range(3):
                part = section(*now, depth_sides[side])
                change = tendency(
                    [turn(value, -WIDE) for value in part["up"]],
                    [turn(value, WIDE) for value in part["down"]],
                    [turn(value, -1) for value in part["back"]],
                    [turn(value, 1) for value in part["ahead"]],
                    part["here"],
                )
                now = [combine(stage, first[f], now[f], land_sides[side] * change[f]) for f in range(FIELDS)]
            done.append(now)
        edges = [jnp.where(column >= HALO, done[0][f], done[1][f]) for f in range(FIELDS)]
        for f in range(FIELDS):
            edge_ref[f, m] = edges[f]
        at = pl.ds(pl.multiple_of(m * 8, 8), 8)
        heights = [mended(edges[0], r, final_row(0, r, at, inner_ref, outer_ref)) for r in range(ROWS)]
        for part in range(OBS // COLS):
            cut = slice(part * COLS, (part + 1) * COLS)
            got = jnp.zeros((8, COLS), F32)
            for r in range(ROWS):
                picked = jnp.take_along_axis(heights[r], cell_col[:, cut], axis=1)
                got = jnp.where(cell_row[:, cut] == r, picked, got)
            seen[at, cut] = got
        return carry

    lax.fori_loop(0, BLOCKS, strip, 0, unroll=4)
    everything = seen[...]
    obs_mean = jnp.sum(everything, axis=0, keepdims=True) * (1.0 / MEMBERS)
    scaled = (everything - obs_mean) * weight_ref[0:1, :]
    innovation = (weight_ref[2:3, :] - obs_mean) * weight_ref[1:2, :]
    product = lax.dot_general(
        jnp.concatenate([scaled, jnp.broadcast_to(innovation, (8, OBS))], axis=0),
        scaled,
        (((1,), (1,)), ((), ())),
        precision=lax.Precision.HIGHEST,
        preferred_element_type=F32,
    )
    half = MEMBERS // 2
    whole = jnp.concatenate([product, jnp.zeros((MEMBERS + 8, COLS - MEMBERS), F32)], axis=1)
    lane, sub = lanes(), grid_sub()
    folded = []
    diagonal = jnp.zeros((8, COLS), F32)
    for k in range(half // 8):
        upper = whole[k * 8 : k * 8 + 8]
        lower = turn(whole[half + k * 8 : half + k * 8 + 8], -half)
        folded.append(jnp.where((lane >= half) | (lane >= sub + 8 * k), upper, lower))
        diagonal = diagonal + jnp.where(lane == sub + 8 * k, lower, 0.0)
    for k in range(2):
        part_ref[k * 8 : k * 8 + 8, :] = jnp.where(lane < MEMBERS, folded[k], turn(folded[k + 2], MEMBERS))
    diagonal = turn(spread(jnp.sum(diagonal, axis=0, keepdims=True)), MEMBERS)
    part_ref[16:, :] = jnp.where(lane < MEMBERS, whole[MEMBERS:], diagonal)


def deviate(edge_ref, inner_ref, outer_ref, big_ref, small_ref, mean_ref):
    for f in range(FIELDS):
        for r in range(ROWS):
            rows = []
            for m in range(BLOCKS):
                at = slice(m * 8, m * 8 + 8)
                rows.append(mended(edge_ref[f, m], r, final_row(f, r, at, inner_ref, outer_ref)))
            value = jnp.concatenate(rows, axis=0)
            mean = jnp.sum(value, axis=0, keepdims=True) * (1.0 / MEMBERS)
            k = f * ROWS + r
            mean_ref[k : k + 1, :] = mean
            value = value - mean
            big = value.astype(BF16)
            big_ref[f, r] = big
            small_ref[f, r] = (value - big.astype(F32)).astype(BF16)


def column_of(value, j):
    return jnp.broadcast_to(value[:, j : j + 1], (8, COLS))


def inverse_factor(sum_ref, flip_ref):
    lane, sub = lanes(), grid_sub()
    half = MEMBERS // 2
    folded = [turn(sum_ref[(k % 2) * 8 : (k % 2) * 8 + 8, :], MEMBERS * (k // 2)) for k in range(4)]
    flip_ref[:, :half] = jnp.transpose(jnp.concatenate(folded, axis=0))
    diagonal = turn(spread(sum_ref[16:17, :]), MEMBERS)
    table = []
    for b in range(BLOCKS):
        k = b % 4
        flipped = flip_ref[k * 8 : k * 8 + 8, :]
        at = sub + 8 * k
        if b < 4:
            value = jnp.where((lane >= at), folded[k], flipped)
        else:
            value = jnp.where(lane < at, folded[k], jnp.where(lane > at, flipped, diagonal))
            value = jnp.where(lane < half, flip_ref[b * 8 : b * 8 + 8, :], turn(value, half))
        one = (lane == sub + 8 * b) | (lane == sub + 8 * b + MEMBERS)
        table.append(jnp.where(lane < MEMBERS, value, 0.0) + jnp.where(one, 1.0, 0.0))
    for b in range(BLOCKS):
        rows = [spread(table[b][s : s + 1, :]) for s in range(8)]
        entry = {(s, t): column_of(rows[s], 8 * b + t) for s in range(8) for t in range(s, 8)}
        over = []
        for s in range(8):
            over.append(1.0 / entry[s, s])
            for t in range(s + 1, 8):
                factor = entry[s, t] * over[s]
                for q in range(t, 8):
                    entry[t, q] = entry[t, q] - factor * entry[s, q]
                rows[t] = rows[t] - factor * rows[s]
        for i in range(b + 1, BLOCKS):
            column = [column_of(table[i], 8 * b + s) for s in range(8)]
            for s in range(8):
                column[s] = column[s] * over[s]
                for t in range(s + 1, 8):
                    column[t] = column[t] - column[s] * entry[s, t]
                table[i] = table[i] - column[s] * rows[s]
        for s in range(8):
            table[b] = jnp.where(sub == s, rows[s] * lax.rsqrt(entry[s, s]), table[b])
    return [jnp.where(lane < MEMBERS, turn(value, MEMBERS), 0.0) for value in table]


def analyse(parts_ref, big_ref, small_ref, mean_ref, out_hbm, out_ref, flip_ref, sum_ref, sems):
    sums = [parts_ref[i] for i in range(parts_ref.shape[0])]
    while len(sums) > 1:
        sums = [a + b for a, b in zip(sums[::2], sums[1::2])]
    sum_ref[...] = sums[0]
    inverse = inverse_factor(sum_ref, flip_ref)
    projection = spread(sum_ref[16:17, :])
    weights = jnp.zeros((8, COLS), F32)
    for b in range(BLOCKS):
        weights = weights + inverse[b] * jnp.sum(inverse[b] * projection, axis=1, keepdims=True)
    weights = jnp.sum(weights, axis=0, keepdims=True) / np.sqrt(np.float32(MEMBERS - 1))
    transform = jnp.concatenate(inverse, axis=0)[:, :MEMBERS] + weights[:, :MEMBERS]
    high = transform.astype(BF16)
    low = (transform - high.astype(F32)).astype(BF16)
    taps = jnp.concatenate([high, low, high], axis=1)
    stores = []
    for f in range(FIELDS):
        for r in range(0, ROWS, 2):
            big = jnp.concatenate([big_ref[f, r], big_ref[f, r + 1]], axis=1)
            small = jnp.concatenate([small_ref[f, r], small_ref[f, r + 1]], axis=1)
            mixed = jnp.dot(taps, jnp.concatenate([big, big, small], axis=0), preferred_element_type=F32)
            for q in range(2):
                k = f * ROWS + r + q
                out_ref[pl.ds(f * MEMBERS * ROWS + r + q, MEMBERS, stride=ROWS), :] = (
                    mean_ref[k : k + 1, :] + mixed[:, q * COLS : (q + 1) * COLS]
                )
        cut = pl.ds(f * MEMBERS * ROWS, MEMBERS * ROWS)
        stores.append(pltpu.make_async_copy(out_ref.at[cut], out_hbm.at[cut], sems.at[f]))
        stores[-1].start()
    for store in stores:
        store.wait()


def swap(value, axis, pairs):
    return lax.ppermute(value, axis, [(a, b) for a, b in pairs] + [(b, a) for a, b in pairs])


def pairs_of(count, first, wrap=False):
    return [(i, (i + 1) % count) for i in range(first, count if wrap else count - 1, 2)]


def duplicate(part_ref, other_ref, out_ref):
    value = part_ref[...] + other_ref[...]
    for i in range(out_ref.shape[0]):
        out_ref[i] = value


def gathered(part):
    gx, gy = lax.axis_size("gx"), lax.axis_size("gy")
    for flip in (1, 3, 5, 13):
        pairs = [(i * gy + j, (i ^ flip) * gy + j) for i in range(gx) for j in range(gy)]
        other = lax.ppermute(part, ("gx", "gy"), pairs)
        if flip < 13:
            part = part + other
    groups = [[(y * 16 + i) * gy + x for y in range(gx // 16) for x in range(gy)] for i in range(16)]
    (copies,) = call(duplicate, (shape(len(groups[0]), *part.shape),), vmem(2))(part, other)
    return lax.all_to_all(copies, ("gx", "gy"), 0, 0, axis_index_groups=groups)


def shape(*sizes, dtype=F32):
    return jax.ShapeDtypeStruct(sizes, dtype)


def hbm(count):
    return [pl.BlockSpec(memory_space=pltpu.HBM)] * count


def call(body, outs, ins, scratch=(), out_specs=None, moved=2 * 2**20):
    return pl.pallas_call(
        body,
        out_shape=outs,
        in_specs=ins,
        out_specs=out_specs or tuple(vmem(len(outs))),
        scratch_shapes=scratch,
        compiler_params=pltpu.CompilerParams(vmem_limit_bytes=8 * 2**20),
        cost_estimate=pl.CostEstimate(flops=0, transcendentals=0, bytes_accessed=moved),
    )


def local(members_state, depth_level, land_mask, obs_cells, obs_values, obs_error):
    x = members_state.reshape(FIELDS * MEMBERS * ROWS, COLS)
    dma = pltpu.SemaphoreType.DMA
    payload = shape(EDGE + 8, COLS)
    start, geo, near, far = call(
        arrange,
        (shape(FIELDS, ROWS, MEMBERS, COLS), shape(2, ROWS, COLS), payload, payload),
        hbm(3),
        [
            pltpu.VMEM(x.shape, F32), pltpu.VMEM((ROWS, COLS), jnp.int32), pltpu.VMEM((ROWS, COLS), jnp.int32),
            dma((5,)),
        ],
    )(*[pltpu.with_memory_space_constraint(value, pltpu.HBM) for value in (x, depth_level, land_mask)])
    far = swap(far, "gx", pairs_of(64, 1))
    near = swap(near, "gx", pairs_of(64, 0))
    own = shape(FIELDS * BLOCKS + 2, 8, COLS)
    own_left, own_right, c1, c2, c3 = call(
        interior,
        (own, own) + tuple(shape(FIELDS, count, MEMBERS, COLS) for count in (6, 4, 2)),
        vmem(2),
        [pltpu.VMEM((2, ROWS, 8, COLS), F32)],
        moved=8 * 2**20,
    )(start, geo)
    tile = shape(BLOCKS + 1, 8, COLS)
    outside = shape(FIELDS, 2 * HALO, MEMBERS, COLS)
    halo, wide, left, right, a, b = call(
        strips, (outside, shape(2, EXT, COLS), own, own, tile, tile), vmem(5)
    )(near, far, geo, own_left, own_right)
    b = swap(b, "gy", pairs_of(4, 1, wrap=True))
    a = swap(a, "gy", pairs_of(4, 0))
    rows = pltpu.VMEM((FIELDS, EXT, 8, COLS), F32)
    line = pltpu.VMEM((1, OBS), F32)
    last, cell, weight = call(
        outer,
        (outside, jax.ShapeDtypeStruct((2, 8, OBS), jnp.int32), shape(8, OBS)),
        vmem(5) + hbm(3),
        [
            pltpu.VMEM((2, EXT, 8, COLS), F32), rows, rows,
            pltpu.VMEM((1, OBS), jnp.int32), line, line, dma((3,)),
        ],
        moved=6 * 2**20,
    )(
        start, halo, wide, c1, c2,
        *[
            pltpu.with_memory_space_constraint(value.reshape(1, OBS), pltpu.HBM)
            for value in (obs_cells, obs_values, obs_error)
        ],
    )
    edge, part = call(
        observe,
        (shape(FIELDS, BLOCKS, 8, COLS), shape(24, COLS)),
        vmem(8),
        [pltpu.VMEM((MEMBERS, OBS), F32)],
    )(left, right, a, b, c3, last, cell, weight)
    half = shape(FIELDS, ROWS, MEMBERS, COLS, dtype=BF16)
    big, small, mean = call(
        deviate, (half, half, shape(FIELDS * ROWS, COLS)), vmem(3), moved=4 * 2**20
    )(edge, c3, last)
    (out,) = call(
        analyse,
        (shape(*x.shape),),
        vmem(4),
        [pltpu.VMEM(x.shape, F32), pltpu.VMEM((COLS, COLS), F32), pltpu.VMEM((24, COLS), F32), dma((FIELDS,))],
        out_specs=tuple(hbm(1)),
    )(gathered(part), big, small, mean)
    return out.reshape(FIELDS, MEMBERS, ROWS, COLS)


def solution(mesh):
    placed = (
        P(None, None, "gx", "gy"),
        P("gx", "gy"),
        P("gx", "gy"),
        P("gx", "gy", None),
        P("gx", "gy", None),
        P("gx", "gy", None),
    )

    return jax.shard_map(local, mesh=mesh, in_specs=placed, out_specs=P(None, None, "gx", "gy"), check_vma=False)
```

```python
import jax
import jax.numpy as jnp
import numpy as np
from jax import lax
from jax.experimental import pallas as pl
from jax.experimental.pallas import tpu as pltpu
from jax.sharding import PartitionSpec as P

F32 = jnp.float32
BF16 = jnp.bfloat16
MEMBERS = 64
BLOCKS = 8
ROWS = 8
COLS = 128
HALO = 3
EXT = ROWS + 2 * HALO
WIDE = 9
OBS = 256
FIELDS = 3
EDGE = FIELDS * HALO * MEMBERS


def vmem(count):
    return [pl.BlockSpec(memory_space=pltpu.VMEM)] * count


def lanes():
    return lax.broadcasted_iota(jnp.int32, (8, COLS), 1)


def grid_sub():
    return lax.broadcasted_iota(jnp.int32, (8, COLS), 0)


def turn(value, shift):
    shift = shift % COLS
    return value if shift == 0 else pltpu.roll(value, shift, 1)


def spread(row):
    return jnp.broadcast_to(row, (8, COLS))


def arrange(x_hbm, depth_hbm, land_hbm, start_ref, geo_ref, near_ref, far_ref, x_ref, depth_ref, land_ref, sems):
    size = MEMBERS * ROWS
    loads = [
        pltpu.make_async_copy(land_hbm, land_ref, sems.at[0]),
        pltpu.make_async_copy(depth_hbm, depth_ref, sems.at[1]),
    ]
    for f in range(FIELDS):
        cut = pl.ds(f * size, size)
        loads.append(pltpu.make_async_copy(x_hbm.at[cut], x_ref.at[cut], sems.at[2 + f]))
    for load in loads:
        load.start()
    odd = lax.rem(lax.axis_index("gx"), 2)
    loads[0].wait()
    loads[1].wait()
    land = land_ref[...].astype(F32)
    geo_ref[0] = 0.125 * depth_ref[...].astype(F32) * land
    geo_ref[1] = land
    low = (ROWS - HALO) * (1 - odd)
    sends = ((near_ref, low), (far_ref, (ROWS - HALO) - low))
    for target, first in sends:
        for g in range(2):
            for r in range(HALO):
                at = EDGE + g * HALO + r
                target[at : at + 1, :] = geo_ref[g, pl.ds(first + r, 1), :]
        target[EDGE + 6 : EDGE + 8, :] = jnp.zeros((2, COLS), F32)
    for f in range(FIELDS):
        loads[2 + f].wait()
        for r in range(ROWS):
            value = x_ref[pl.ds(f * size + r, MEMBERS, stride=ROWS), :]
            start_ref[f, r] = value * land[r : r + 1, :]
        for target, first in sends:
            for r in range(HALO):
                at = (f * HALO + r) * MEMBERS
                target[at : at + MEMBERS, :] = start_ref[f, first + r]


def own_columns(row_of, rows, left, right):
    lane = lanes()
    shifted = lax.rem(lane + HALO, COLS)
    for r in rows:
        value = turn(row_of(r), WIDE * r + HALO)
        left = jnp.where((lane // WIDE == r) & (lax.rem(lane, WIDE) >= HALO), value, left)
        right = jnp.where((shifted // WIDE == r) & (lax.rem(shifted, WIDE) < 2 * HALO), value, right)
    return left, right


def interior(start_ref, geo_ref, left_ref, right_ref, c1_ref, c2_ref, c3_ref, geo):
    for r in range(ROWS):
        geo[0, r] = spread(geo_ref[0, r : r + 1, :])
        geo[1, r] = spread(0.3 * geo_ref[1, r : r + 1, :])
    blank = jnp.zeros((8, COLS), F32)
    inside = range(HALO, HALO + ROWS)

    def block(m, carry):
        at = pl.ds(pl.multiple_of(m * 8, 8), 8)
        for f in range(FIELDS):
            place = f * BLOCKS + m
            left_ref[place], right_ref[place] = own_columns(
                lambda r: start_ref[f, r - HALO, at, :], inside, blank, blank
            )

        def first(f, r):
            return start_ref[f, r, at, :]

        refs = (c1_ref, c2_ref, c3_ref)
        for stage in range(3):
            read = first if stage == 0 else (lambda f, r: refs[stage - 1][f, r - stage, at, :])

            def write(f, r, new):
                refs[stage][f, r - stage - 1, at, :] = new

            advance(stage, range(stage + 1, ROWS - stage - 1), first, read, geo, write)
        return carry

    lax.fori_loop(0, BLOCKS, block, 0)
    for g in range(2):
        place = FIELDS * BLOCKS + g
        left_ref[place], right_ref[place] = own_columns(
            lambda r: spread(geo_ref[g, r - HALO : r - HALO + 1, :]), inside, blank, blank
        )


def strips(near_ref, far_ref, geo_ref, own_left, own_right, halo_ref, wide_ref, left_ref, right_ref, a_ref, b_ref):
    odd_x = lax.rem(lax.axis_index("gx"), 2) == 1
    odd_y = lax.rem(lax.axis_index("gy"), 2) == 1
    field = lax.rem(lanes(), WIDE) // HALO
    outside = tuple(range(HALO)) + tuple(range(HALO + ROWS, EXT))

    def halves(cut):
        near, far = near_ref[cut, :], far_ref[cut, :]
        return jnp.where(odd_x, near, far), jnp.where(odd_x, far, near)

    above, below = halves(slice(EDGE, EDGE + 8))
    for g in range(2):
        at = slice(g * HALO, (g + 1) * HALO)
        wide_ref[g, :HALO] = above[at]
        wide_ref[g, HALO : HALO + ROWS] = geo_ref[g]
        wide_ref[g, HALO + ROWS :] = below[at]

    def put(packed, row_of, f, place):
        to_left, to_right = packed
        left, right = own_columns(row_of, outside, own_left[place], own_right[place])
        left_ref[place] = left
        right_ref[place] = right
        to_left = jnp.where(field == f, turn(left, HALO * f - HALO), to_left)
        to_right = jnp.where(field == f, turn(right, HALO * f), to_right)
        return to_left, to_right

    def send(place, packed):
        to_left, to_right = packed
        a_ref[place] = jnp.where(odd_y, to_left, to_right)
        b_ref[place] = jnp.where(odd_y, to_right, to_left)

    def block(m, carry):
        at = pl.ds(pl.multiple_of(m * 8, 8), 8)
        packed = (jnp.zeros((8, COLS), F32),) * 2
        for f in range(FIELDS):
            rows = {}
            for r in range(HALO):
                cut = pl.ds(pl.multiple_of((f * HALO + r) * MEMBERS + m * 8, 8), 8)
                rows[r], rows[r + ROWS + HALO] = halves(cut)
                halo_ref[f, r, at, :] = rows[r]
                halo_ref[f, r + HALO, at, :] = rows[r + ROWS + HALO]
            packed = put(packed, rows.get, f, f * BLOCKS + m)
        send(m, packed)
        return carry

    lax.fori_loop(0, BLOCKS, block, 0, unroll=4)
    packed = (jnp.zeros((8, COLS), F32),) * 2
    for g in range(2):
        packed = put(packed, lambda r: spread(wide_ref[g, r : r + 1, :]), g, FIELDS * BLOCKS + g)
    send(BLOCKS, packed)


def section(h, u, v, depth):
    damp = 0.05 * h
    half = 0.5 * h
    east, north = depth * u, depth * v
    us, vs = 0.05 * u, 0.05 * v
    return dict(
        up=(damp - east, us - half, vs),
        down=(damp + east, us + half, vs),
        back=(damp - north, us, vs - half),
        ahead=(damp + north, us, vs + half),
        here=(-0.2 * h, 0.2 * (v - u), -0.2 * (u + v)),
    )


def tendency(up, down, back, ahead, here):
    return [a + b + c + d + e for a, b, c, d, e in zip(up, down, back, ahead, here)]


def combine(stage, first, old, change):
    new = old + change
    if stage == 0:
        return new
    if stage == 1:
        return 0.75 * first + 0.25 * new
    return (1.0 / 3.0) * first + (2.0 / 3.0) * new


def advance(stage, rows, first, read, geo, write):
    known = {}

    def part_of(r):
        if r not in known:
            known[r] = section(*[read(f, r) for f in range(FIELDS)], geo[0, r])
        return known[r]

    for r in rows:
        mine = part_of(r)
        change = tendency(
            part_of(r + 1)["up"],
            part_of(r - 1)["down"],
            [turn(value, -1) for value in mine["back"]],
            [turn(value, 1) for value in mine["ahead"]],
            mine["here"],
        )
        for f in range(FIELDS):
            write(f, r, combine(stage, first(f, r), read(f, r), geo[1, r] * change[f]))


OUTER = tuple(range(HALO)) + tuple(range(ROWS - HALO, ROWS))


def outer(
    start_ref, halo_ref, wide_ref, c1_ref, c2_ref, cells_hbm, values_hbm, error_hbm,
    last_ref, cell_ref, weight_ref, geo, s1, s2, cells_ref, values_ref, error_ref, sems,
):
    loads = [
        pltpu.make_async_copy(source, target, sems.at[i])
        for i, (source, target) in enumerate(
            ((cells_hbm, cells_ref), (values_hbm, values_ref), (error_hbm, error_ref))
        )
    ]
    for load in loads:
        load.start()
    for r in range(EXT):
        geo[0, r] = spread(wide_ref[0, r : r + 1, :])
        geo[1, r] = spread(0.3 * wide_ref[1, r : r + 1, :])

    def block(m, carry):
        at = pl.ds(pl.multiple_of(m * 8, 8), 8)

        def first(f, r):
            if r < HALO:
                return halo_ref[f, r, at, :]
            if r < HALO + ROWS:
                return start_ref[f, r - HALO, at, :]
            return halo_ref[f, r - ROWS, at, :]

        for stage in range(3):

            def read(f, r):
                if stage == 0:
                    return first(f, r)
                inside = HALO + stage
                if inside <= r < EXT - inside:
                    return (c1_ref, c2_ref)[stage - 1][f, r - inside, at, :]
                return (s1, s2)[stage - 1][f, r]

            def write(f, r, new):
                if stage < 2:
                    (s1, s2)[stage][f, r] = new
                else:
                    last_ref[f, OUTER.index(r - HALO), at, :] = new

            low, high = stage + 1, stage + 1 + HALO
            advance(stage, range(low, high), first, read, geo, write)
            advance(stage, range(EXT - high, EXT - low), first, read, geo, write)
        return carry

    lax.fori_loop(0, BLOCKS, block, 0)
    for load in loads:
        load.wait()
    cell = jnp.broadcast_to(cells_ref[...], (8, OBS))
    cell_ref[0] = cell // COLS
    cell_ref[1] = lax.rem(cell, COLS)
    error = error_ref[...]
    weight_ref[0:1, :] = 1.0 / (error * np.sqrt(np.float32(MEMBERS - 1)))
    weight_ref[1:2, :] = 1.0 / error
    weight_ref[2:3, :] = values_ref[...]


def final_row(f, r, at, inner_ref, outer_ref):
    return outer_ref[f, OUTER.index(r), at, :] if r in OUTER else inner_ref[f, r - HALO, at, :]


def mended(edge, r, value):
    lane = lanes()
    border = (lane < HALO) | (lane >= COLS - HALO)
    return jnp.where(border, turn(edge, -(WIDE * (r + HALO) + HALO)), value)


def observe(
    left_ref, right_ref, a_ref, b_ref, inner_ref, outer_ref, cell_ref, weight_ref, edge_ref, part_ref, seen
):
    place_y = lax.axis_index("gy")
    odd_y = lax.rem(place_y, 2) == 1
    inside = (place_y > 0) & (place_y < lax.axis_size("gy") - 1)
    column = lax.rem(lanes(), WIDE)

    def sides(place, f, own):
        a, b = a_ref[place], jnp.where(inside, b_ref[place], 0.0)
        from_left, from_right = jnp.where(odd_y, a, b), jnp.where(odd_y, b, a)
        left = jnp.where(column < HALO, turn(from_left, -HALO * f), left_ref[own])
        right = jnp.where(
            (column >= HALO) & (column < 2 * HALO), turn(from_right, HALO - HALO * f), right_ref[own]
        )
        return left, right

    depth_sides = sides(BLOCKS, 0, FIELDS * BLOCKS)
    land_sides = [0.3 * value for value in sides(BLOCKS, 1, FIELDS * BLOCKS + 1)]

    cell_row, cell_col = cell_ref[0], cell_ref[1]

    def strip(m, carry):
        fields = [sides(m, f, f * BLOCKS + m) for f in range(FIELDS)]
        done = []
        for side in range(2):
            first = [fields[f][side] for f in range(FIELDS)]
            now = first
            for stage in range(3):
                part = section(*now, depth_sides[side])
                change = tendency(
                    [turn(value, -WIDE) for value in part["up"]],
                    [turn(value, WIDE) for value in part["down"]],
                    [turn(value, -1) for value in part["back"]],
                    [turn(value, 1) for value in part["ahead"]],
                    part["here"],
                )
                now = [combine(stage, first[f], now[f], land_sides[side] * change[f]) for f in range(FIELDS)]
            done.append(now)
        edges = [jnp.where(column >= HALO, done[0][f], done[1][f]) for f in range(FIELDS)]
        for f in range(FIELDS):
            edge_ref[f, m] = edges[f]
        at = pl.ds(pl.multiple_of(m * 8, 8), 8)
        heights = [mended(edges[0], r, final_row(0, r, at, inner_ref, outer_ref)) for r in range(ROWS)]
        for part in range(OBS // COLS):
            cut = slice(part * COLS, (part + 1) * COLS)
            got = jnp.zeros((8, COLS), F32)
            for r in range(ROWS):
                picked = jnp.take_along_axis(heights[r], cell_col[:, cut], axis=1)
                got = jnp.where(cell_row[:, cut] == r, picked, got)
            seen[at, cut] = got
        return carry

    lax.fori_loop(0, BLOCKS, strip, 0, unroll=4)
    everything = seen[...]
    obs_mean = jnp.sum(everything, axis=0, keepdims=True) * (1.0 / MEMBERS)
    scaled = (everything - obs_mean) * weight_ref[0:1, :]
    innovation = (weight_ref[2:3, :] - obs_mean) * weight_ref[1:2, :]
    product = lax.dot_general(
        jnp.concatenate([scaled, jnp.broadcast_to(innovation, (8, OBS))], axis=0),
        scaled,
        (((1,), (1,)), ((), ())),
        precision=lax.Precision.HIGHEST,
        preferred_element_type=F32,
    )
    half = MEMBERS // 2
    whole = jnp.concatenate([product, jnp.zeros((MEMBERS + 8, COLS - MEMBERS), F32)], axis=1)
    lane, sub = lanes(), grid_sub()
    folded = []
    diagonal = jnp.zeros((8, COLS), F32)
    for k in range(half // 8):
        upper = whole[k * 8 : k * 8 + 8]
        lower = turn(whole[half + k * 8 : half + k * 8 + 8], -half)
        folded.append(jnp.where((lane >= half) | (lane >= sub + 8 * k), upper, lower))
        diagonal = diagonal + jnp.where(lane == sub + 8 * k, lower, 0.0)
    for k in range(2):
        part_ref[k * 8 : k * 8 + 8, :] = jnp.where(lane < MEMBERS, folded[k], turn(folded[k + 2], MEMBERS))
    diagonal = turn(spread(jnp.sum(diagonal, axis=0, keepdims=True)), MEMBERS)
    part_ref[16:, :] = jnp.where(lane < MEMBERS, whole[MEMBERS:], diagonal)


def deviate(edge_ref, inner_ref, outer_ref, big_ref, small_ref, mean_ref):
    for f in range(FIELDS):
        for r in range(ROWS):
            rows = []
            for m in range(BLOCKS):
                at = slice(m * 8, m * 8 + 8)
                rows.append(mended(edge_ref[f, m], r, final_row(f, r, at, inner_ref, outer_ref)))
            value = jnp.concatenate(rows, axis=0)
            mean = jnp.sum(value, axis=0, keepdims=True) * (1.0 / MEMBERS)
            k = f * ROWS + r
            mean_ref[k : k + 1, :] = mean
            value = value - mean
            big = value.astype(BF16)
            big_ref[f, r] = big
            small_ref[f, r] = (value - big.astype(F32)).astype(BF16)


def column_of(value, j):
    return jnp.broadcast_to(value[:, j : j + 1], (8, COLS))


def inverse_factor(sum_ref, flip_ref):
    lane, sub = lanes(), grid_sub()
    half = MEMBERS // 2
    folded = [turn(sum_ref[(k % 2) * 8 : (k % 2) * 8 + 8, :], MEMBERS * (k // 2)) for k in range(4)]
    flip_ref[:, :half] = jnp.transpose(jnp.concatenate(folded, axis=0))
    diagonal = turn(spread(sum_ref[16:17, :]), MEMBERS)
    table = []
    for b in range(BLOCKS):
        k = b % 4
        flipped = flip_ref[k * 8 : k * 8 + 8, :]
        at = sub + 8 * k
        if b < 4:
            value = jnp.where((lane >= at), folded[k], flipped)
        else:
            value = jnp.where(lane < at, folded[k], jnp.where(lane > at, flipped, diagonal))
            value = jnp.where(lane < half, flip_ref[b * 8 : b * 8 + 8, :], turn(value, half))
        one = (lane == sub + 8 * b) | (lane == sub + 8 * b + MEMBERS)
        table.append(jnp.where(lane < MEMBERS, value, 0.0) + jnp.where(one, 1.0, 0.0))
    for b in range(BLOCKS):
        rows = [spread(table[b][s : s + 1, :]) for s in range(8)]
        entry = {(s, t): column_of(rows[s], 8 * b + t) for s in range(8) for t in range(s, 8)}
        over = {}
        for s in range(0, 8, 2):
            p, q, r = entry[s, s], entry[s, s + 1], entry[s + 1, s + 1]
            over[s] = 1.0 / (p * r - q * q)
            for t in range(s + 2, 8):
                one = (r * entry[s, t] - q * entry[s + 1, t]) * over[s]
                two = (p * entry[s + 1, t] - q * entry[s, t]) * over[s]
                for k in range(t, 8):
                    entry[t, k] = entry[t, k] - (one * entry[s, k] + two * entry[s + 1, k])
                rows[t] = rows[t] - (one * rows[s] + two * rows[s + 1])
        for i in range(b + 1, BLOCKS):
            column = [column_of(table[i], 8 * b + s) for s in range(8)]
            for s in range(0, 8, 2):
                p, q, r = entry[s, s], entry[s, s + 1], entry[s + 1, s + 1]
                one = (r * column[s] - q * column[s + 1]) * over[s]
                two = (p * column[s + 1] - q * column[s]) * over[s]
                for t in range(s + 2, 8):
                    column[t] = column[t] - (one * entry[s, t] + two * entry[s + 1, t])
                table[i] = table[i] - (one * rows[s] + two * rows[s + 1])
        for s in range(0, 8, 2):
            p, q, r = entry[s, s], entry[s, s + 1], entry[s + 1, s + 1]
            inverse = 1.0 / p
            last = (rows[s + 1] - (q * inverse) * rows[s]) * lax.rsqrt((p * r - q * q) * inverse)
            table[b] = jnp.where(sub == s, rows[s] * lax.rsqrt(p), table[b])
            table[b] = jnp.where(sub == s + 1, last, table[b])
    return [jnp.where(lane < MEMBERS, turn(value, MEMBERS), 0.0) for value in table]


def analyse(parts_ref, big_ref, small_ref, mean_ref, out_hbm, out_ref, flip_ref, sum_ref, sems):
    sums = [parts_ref[i] for i in range(parts_ref.shape[0])]
    while len(sums) > 1:
        sums = [a + b for a, b in zip(sums[::2], sums[1::2])]
    sum_ref[...] = sums[0]
    inverse = inverse_factor(sum_ref, flip_ref)
    projection = spread(sum_ref[16:17, :])
    weights = jnp.zeros((8, COLS), F32)
    for b in range(BLOCKS):
        weights = weights + inverse[b] * jnp.sum(inverse[b] * projection, axis=1, keepdims=True)
    weights = jnp.sum(weights, axis=0, keepdims=True) / np.sqrt(np.float32(MEMBERS - 1))
    transform = jnp.concatenate(inverse, axis=0)[:, :MEMBERS] + weights[:, :MEMBERS]
    high = transform.astype(BF16)
    low = (transform - high.astype(F32)).astype(BF16)
    taps = jnp.concatenate([high, low, high], axis=1)
    stores = []
    for f in range(FIELDS):
        for r in range(0, ROWS, 2):
            big = jnp.concatenate([big_ref[f, r], big_ref[f, r + 1]], axis=1)
            small = jnp.concatenate([small_ref[f, r], small_ref[f, r + 1]], axis=1)
            mixed = jnp.dot(taps, jnp.concatenate([big, big, small], axis=0), preferred_element_type=F32)
            for q in range(2):
                k = f * ROWS + r + q
                out_ref[pl.ds(f * MEMBERS * ROWS + r + q, MEMBERS, stride=ROWS), :] = (
                    mean_ref[k : k + 1, :] + mixed[:, q * COLS : (q + 1) * COLS]
                )
        cut = pl.ds(f * MEMBERS * ROWS, MEMBERS * ROWS)
        stores.append(pltpu.make_async_copy(out_ref.at[cut], out_hbm.at[cut], sems.at[f]))
        stores[-1].start()
    for store in stores:
        store.wait()


def swap(value, axis, pairs):
    return lax.ppermute(value, axis, [(a, b) for a, b in pairs] + [(b, a) for a, b in pairs])


def pairs_of(count, first, wrap=False):
    return [(i, (i + 1) % count) for i in range(first, count if wrap else count - 1, 2)]


def duplicate(part_ref, other_ref, out_ref):
    value = part_ref[...] + other_ref[...]
    for i in range(out_ref.shape[0]):
        out_ref[i] = value


def gathered(part):
    gx, gy = lax.axis_size("gx"), lax.axis_size("gy")
    for flip in (1, 13, 5, 3):
        pairs = [(i * gy + j, (i ^ flip) * gy + j) for i in range(gx) for j in range(gy)]
        other = lax.ppermute(part, ("gx", "gy"), pairs)
        if flip != 3:
            part = part + other
    groups = [[(y * 16 + i) * gy + x for y in range(gx // 16) for x in range(gy)] for i in range(16)]
    (copies,) = call(duplicate, (shape(len(groups[0]), *part.shape),), vmem(2))(part, other)
    return lax.all_to_all(copies, ("gx", "gy"), 0, 0, axis_index_groups=groups)


def shape(*sizes, dtype=F32):
    return jax.ShapeDtypeStruct(sizes, dtype)


def hbm(count):
    return [pl.BlockSpec(memory_space=pltpu.HBM)] * count


def call(body, outs, ins, scratch=(), out_specs=None, moved=2 * 2**20):
    return pl.pallas_call(
        body,
        out_shape=outs,
        in_specs=ins,
        out_specs=out_specs or tuple(vmem(len(outs))),
        scratch_shapes=scratch,
        compiler_params=pltpu.CompilerParams(vmem_limit_bytes=8 * 2**20),
        cost_estimate=pl.CostEstimate(flops=0, transcendentals=0, bytes_accessed=moved),
    )


def local(members_state, depth_level, land_mask, obs_cells, obs_values, obs_error):
    x = members_state.reshape(FIELDS * MEMBERS * ROWS, COLS)
    dma = pltpu.SemaphoreType.DMA
    payload = shape(EDGE + 8, COLS)
    start, geo, near, far = call(
        arrange,
        (shape(FIELDS, ROWS, MEMBERS, COLS), shape(2, ROWS, COLS), payload, payload),
        hbm(3),
        [
            pltpu.VMEM(x.shape, F32), pltpu.VMEM((ROWS, COLS), jnp.int32), pltpu.VMEM((ROWS, COLS), jnp.int32),
            dma((5,)),
        ],
    )(*[pltpu.with_memory_space_constraint(value, pltpu.HBM) for value in (x, depth_level, land_mask)])
    far = swap(far, "gx", pairs_of(64, 1))
    near = swap(near, "gx", pairs_of(64, 0))
    own = shape(FIELDS * BLOCKS + 2, 8, COLS)
    own_left, own_right, c1, c2, c3 = call(
        interior,
        (own, own) + tuple(shape(FIELDS, count, MEMBERS, COLS) for count in (6, 4, 2)),
        vmem(2),
        [pltpu.VMEM((2, ROWS, 8, COLS), F32)],
        moved=8 * 2**20,
    )(start, geo)
    tile = shape(BLOCKS + 1, 8, COLS)
    outside = shape(FIELDS, 2 * HALO, MEMBERS, COLS)
    halo, wide, left, right, a, b = call(
        strips, (outside, shape(2, EXT, COLS), own, own, tile, tile), vmem(5)
    )(near, far, geo, own_left, own_right)
    b = swap(b, "gy", pairs_of(4, 1, wrap=True))
    a = swap(a, "gy", pairs_of(4, 0))
    rows = pltpu.VMEM((FIELDS, EXT, 8, COLS), F32)
    line = pltpu.VMEM((1, OBS), F32)
    last, cell, weight = call(
        outer,
        (outside, jax.ShapeDtypeStruct((2, 8, OBS), jnp.int32), shape(8, OBS)),
        vmem(5) + hbm(3),
        [
            pltpu.VMEM((2, EXT, 8, COLS), F32), rows, rows,
            pltpu.VMEM((1, OBS), jnp.int32), line, line, dma((3,)),
        ],
        moved=6 * 2**20,
    )(
        start, halo, wide, c1, c2,
        *[
            pltpu.with_memory_space_constraint(value.reshape(1, OBS), pltpu.HBM)
            for value in (obs_cells, obs_values, obs_error)
        ],
    )
    edge, part = call(
        observe,
        (shape(FIELDS, BLOCKS, 8, COLS), shape(24, COLS)),
        vmem(8),
        [pltpu.VMEM((MEMBERS, OBS), F32)],
    )(left, right, a, b, c3, last, cell, weight)
    half = shape(FIELDS, ROWS, MEMBERS, COLS, dtype=BF16)
    big, small, mean = call(
        deviate, (half, half, shape(FIELDS * ROWS, COLS)), vmem(3), moved=4 * 2**20
    )(edge, c3, last)
    (out,) = call(
        analyse,
        (shape(*x.shape),),
        vmem(4),
        [pltpu.VMEM(x.shape, F32), pltpu.VMEM((COLS, COLS), F32), pltpu.VMEM((24, COLS), F32), dma((FIELDS,))],
        out_specs=tuple(hbm(1)),
    )(gathered(part), big, small, mean)
    return out.reshape(FIELDS, MEMBERS, ROWS, COLS)


def solution(mesh):
    placed = (
        P(None, None, "gx", "gy"),
        P("gx", "gy"),
        P("gx", "gy"),
        P("gx", "gy", None),
        P("gx", "gy", None),
        P("gx", "gy", None),
    )

    return jax.shard_map(local, mesh=mesh, in_specs=placed, out_specs=P(None, None, "gx", "gy"), check_vma=False)
```
